32 devices in a mesh: dp: 4 (over x, core), wide: 8 (over z, y).
Axes of the slice: x: 2, y: 2, z: 4, core: 2. Of those that a mesh axis runs over, the one named last changes fastest.
Arguments:
- real_images: bfloat16 [384, 8, 8, 640], P(('dp', 'wide')), may hold values from -6 to 6
- replay_chains: bfloat16 [384, 8, 8, 640], P(('dp', 'wide')), may hold values from -1 to 1
- langevin_noise: bfloat16 [2, 384, 8, 8, 640], P(None, ('dp', 'wide')), may hold values from -16 to 16
- real_cot: bfloat16 [384, 8, 8, 640], P(('dp', 'wide')), may hold values from -6 to 6
- chain_cot: bfloat16 [384, 8, 8, 640], P(('dp', 'wide')), may hold values from -6 to 6
- kernel_one: bfloat16 [3, 3, 640, 640], P(None, None, 'wide'), may hold values from -0.125 to 0.125
- bias_one: bfloat16 [640], P('wide'), may hold values from -3 to 3
- kernel_two: bfloat16 [3, 3, 640, 640], P(None, None, 'wide'), may hold values from -0.125 to 0.125
- bias_two: bfloat16 [640], P('wide'), may hold values from -3 to 3
Outputs:
- block_output: float32 [384, 8, 8, 640], P(('dp', 'wide'))
- input_grad: float32 [384, 8, 8, 640], P(('dp', 'wide'))
- final_samples: float32 [384, 8, 8, 640], P(('dp', 'wide'))
- kernel_one_grad: float32 [3, 3, 640, 640], P(None, None, 'wide')
- bias_one_grad: float32 [640], P('wide')
- kernel_two_grad: float32 [3, 3, 640, 640], P(None, None, 'wide')
- bias_two_grad: float32 [640], P('wide')
The draws below stay inside these ranges and needn't reach their ends.
All inputs are finite; a program needn't handle non-finite values.
Results may differ from the reference program's by a relative error of at most 0.015.
The reference program's roundings to bfloat16 on the way count: a program that leaves them out, or rounds other values in their place, can miss the bound.
Values may be sent and summed in bfloat16 or wider, within the bound.
A program may use at most 256 MiB of HBM per device.

```python
import jax
import jax.numpy as jnp
from jax import lax

C = 640
MAP = 8
STEPS = 2
IMG_DEV = 12
IMAGES = 384


def raised(values, stream_key, source, target, parts, factor):
    def block_of(axis_at):
        return (jnp.arange(values.shape[axis_at]) // (values.shape[axis_at] // parts)).reshape((-1,) + (1,) * (values.ndim - 1 - axis_at))

    near = jax.random.permutation(stream_key, parts)[block_of(target)]
    second = (block_of(target) + parts // 2) % parts
    return jnp.where((block_of(source) == near) | (block_of(source) == second), factor * values, values)


def block_levels(stream_key, shape, pieces, least, top_value):
    loudness = 1.0
    for dim, shards_of in pieces:
        steps = jax.random.uniform(jax.random.fold_in(jax.random.fold_in(stream_key, 6), dim), (shards_of,), jnp.float32, least / len(pieces), top_value / len(pieces))
        loudness = loudness * jnp.repeat(jnp.exp(steps), shape[dim] // shards_of).reshape((-1,) + (1,) * (len(shape) - 1 - dim))
    return loudness


def normal_values(stream_key, extent, spread, limit, cuts=(), held_as=jnp.bfloat16):
    level = block_levels(stream_key, extent, cuts, -0.22, 0.18) if cuts else 1.0
    entries = jax.random.normal(stream_key, extent, jnp.float32) * spread * level
    return jnp.minimum(jnp.maximum(entries, -limit), limit).astype(held_as)


def noise_with(own_key, dims, width, bound, split, heavy, kind=jnp.bfloat16):
    entries = width * jax.random.normal(own_key, dims, jnp.float32)
    if split:
        entries = entries * block_levels(own_key, dims, split, -0.22, 0.18)
    return jnp.clip(raised(entries, jax.random.fold_in(own_key, 3), *heavy), -bound, bound).astype(kind)


def setup_inputs(seed: int = 0) -> dict:
    seeds = jax.random.split(jax.random.key(seed), 10)
    return {
        "real_images": noise_with(seeds[0], (IMAGES, MAP, MAP, C), 1.0, 6.0, ((0, 32),), (0, 3, 32, 2.75)),
        "replay_chains": jnp.clip(jax.random.uniform(seeds[1], (IMAGES, MAP, MAP, C), jnp.float32, -1.0, 1.0) * block_levels(seeds[1], (IMAGES, MAP, MAP, C), ((0, 32),), -0.4, 0.0), -1.0, 1.0).astype(jnp.bfloat16),
        "langevin_noise": normal_values(seeds[2], (STEPS, IMAGES, MAP, MAP, C), 4.0, 16.0, ((1, 32),)),
        "real_cot": normal_values(seeds[3], (IMAGES, MAP, MAP, C), 1.0, 6.0, ((0, 32),)),
        "chain_cot": normal_values(seeds[4], (IMAGES, MAP, MAP, C), 1.0, 6.0, ((0, 32),)),
        "kernel_one": normal_values(seeds[5], (3, 3, C, C), (4 * C) ** -0.5, 0.125, ((2, 8),)),
        "bias_one": normal_values(seeds[6], (C,), 0.5, 3.0, ((0, 8),)),
        "kernel_two": normal_values(seeds[7], (3, 3, C, C), (4 * C) ** -0.5, 0.125, ((2, 8),)),
        "bias_two": normal_values(seeds[8], (C,), 0.5, 3.0, ((0, 8),)),
    }


@jax.custom_vjp
def low(v):
    return lax.optimization_barrier(v.astype(jnp.bfloat16)).astype(jnp.float32)

@jax.custom_vjp
def low_back(v):
    return v

def low_keep(v):
    return (low(v), None)

def low_pass(kept, grad):
    return (grad,)

def back_keep(v):
    return (v, None)

def back_low(kept, grad):
    return (low(grad),)
low.defvjp(low_keep, low_pass)
low_back.defvjp(back_keep, back_low)

def leaky_relu(values):
    return jnp.where(values > 0, values, 0.2 * values)

def conv_layer(activation, kernel, bias_row):
    result = lax.conv_general_dilated(activation, kernel, (1, 1), 'SAME', dimension_numbers=('NHWC', 'HWIO', 'NHWC'), precision=lax.Precision.HIGHEST)
    return result + bias_row

def residual_block(inputs_now, params):
    lower_act = low(leaky_relu(inputs_now))
    hidden = low_back(conv_layer(lower_act, params[0], params[1]))
    upper_act = low(leaky_relu(hidden))
    return inputs_now + low_back(conv_layer(upper_act, params[2], params[3]))

def reference(real_images, replay_chains, langevin_noise, real_cot, chain_cot, kernel_one, bias_one, kernel_two, bias_two):
    params = (kernel_one.astype(jnp.float32), bias_one.astype(jnp.float32), kernel_two.astype(jnp.float32), bias_two.astype(jnp.float32))
    groups = real_images.shape[0] // IMG_DEV

    def blocked(values):
        values = values.astype(jnp.float32)
        return values.reshape((groups, IMG_DEV) + values.shape[1:])
    noise_blocks = jnp.moveaxis(langevin_noise.astype(jnp.float32).reshape((STEPS, groups, IMG_DEV) + langevin_noise.shape[2:]), 1, 0)

    def langevin(inputs):
        chain_state, cotangent, step_noise = inputs
        for step_index in range(STEPS):

            def energy(values):
                return residual_block(values, params)
            _, pullback = jax.vjp(energy, chain_state)
            pull_grad, = pullback(cotangent)
            chain_state = chain_state - pull_grad + 0.01 * step_noise[step_index]
        return chain_state
    samples = lax.map(langevin, (blocked(replay_chains), blocked(chain_cot), noise_blocks))

    def accumulate(totals, inputs):
        images_now, real_grad_in, sample_now, chain_grad_in = inputs
        output, pull_real = jax.vjp(residual_block, images_now, params)
        image_grad, real_terms = pull_real(real_grad_in)
        _, pull_sample = jax.vjp(residual_block, sample_now, params)
        _, sample_terms = pull_sample(-chain_grad_in)
        totals = tuple((running + real_term + sample_term for running, real_term, sample_term in zip(totals, real_terms, sample_terms)))
        return (totals, (output, image_grad))
    initial = tuple((jnp.zeros_like(weight_now) for weight_now in params))
    totals, (outputs, image_grads) = lax.scan(accumulate, initial, (blocked(real_images), blocked(real_cot), samples, blocked(chain_cot)))
    return (outputs.reshape(real_images.shape), image_grads.reshape(real_images.shape), samples.reshape(replay_chains.shape), totals[0], totals[1], totals[2], totals[3])
```

```python
import functools

import jax
import jax.numpy as jnp
from jax import lax
from jax.experimental import pallas as pl
from jax.experimental.pallas import tpu as pltpu
from jax.sharding import PartitionSpec as P

F32 = jnp.float32
BF16 = jnp.bfloat16
MESH = pl.DeviceIdType.MESH


def leaky_relu(values):
    return jnp.where(values > 0, values, 0.2 * values)


def leak_slope(values):
    return jnp.where(values > 0, 1.0, 0.2).astype(F32)


def tap_patches(activation):
    batch_size, height, map_width, channels = activation.shape
    padded = jnp.pad(activation, ((0, 0), (1, 1), (1, 1), (0, 0)))
    tap_list = [
        padded[:, row_off : row_off + height, col_off : col_off + map_width, :]
        for row_off in range(3)
        for col_off in range(3)
    ]
    return jnp.stack(tap_list, axis=3).reshape(batch_size * height * map_width, 9 * channels)


def conv_apply(activation, kernel_mat, bias_row):
    result = jnp.dot(tap_patches(activation), kernel_mat, preferred_element_type=F32)
    return result.reshape(activation.shape[:3] + (kernel_mat.shape[1],)) + bias_row.astype(F32)


def conv_back(gradient, kernel_mat):
    batch_size, height, map_width, channels = gradient.shape
    in_channels = kernel_mat.shape[0] // 9
    spread = lax.dot_general(
        gradient.reshape(-1, channels), kernel_mat, (((1,), (1,)), ((), ())), preferred_element_type=F32
    )
    spread = spread.reshape(batch_size, height, map_width, 9, in_channels)
    summed = jnp.zeros((batch_size, height + 2, map_width + 2, in_channels), F32)
    for row_off in range(3):
        for col_off in range(3):
            summed = summed + jnp.pad(
                spread[:, :, :, 3 * row_off + col_off, :],
                ((0, 0), (row_off, 2 - row_off), (col_off, 2 - col_off), (0, 0)),
            )
    return summed[:, 1 : height + 1, 1 : map_width + 1, :]


def kernel_partial(activation, gradient):
    channels = gradient.shape[3]
    return lax.dot_general(
        tap_patches(activation),
        gradient.reshape(-1, channels),
        (((0,), (0,)), ((), ())),
        preferred_element_type=F32,
    )


def plain_local(real_images, replay_chains, langevin_noise, real_cot, chain_cot, kernel_one, bias_one, kernel_two, bias_two):
    def whole(kernel):
        gathered = lax.all_gather(kernel, "wide", axis=2, tiled=True)
        return gathered.reshape(9 * gathered.shape[2], gathered.shape[3])

    first, second = whole(kernel_one), whole(kernel_two)
    first_bias = lax.all_gather(bias_one, "wide", axis=0, tiled=True)
    second_bias = lax.all_gather(bias_two, "wide", axis=0, tiled=True)

    def hidden_of(values):
        lower = leaky_relu(values).astype(BF16)
        return lower, conv_apply(lower, first, first_bias)

    def x_grad(values, cot, hidden_grad):
        return cot.astype(F32) + leak_slope(values) * conv_back(hidden_grad, first)

    chain_inner = conv_back(chain_cot, second)
    state = replay_chains.astype(F32)
    for step_index in range(langevin_noise.shape[0]):
        _, hidden = hidden_of(state)
        hidden_grad = (chain_inner * leak_slope(hidden)).astype(BF16)
        state = state - x_grad(state, chain_cot, hidden_grad) + 0.01 * langevin_noise[step_index].astype(F32)
    real = real_images.astype(F32)
    real_lower, real_hidden = hidden_of(real)
    real_upper = leaky_relu(real_hidden).astype(BF16)
    block_output = real + conv_apply(real_upper, second, second_bias)
    sample_lower, sample_hidden = hidden_of(state)
    sample_upper = leaky_relu(sample_hidden).astype(BF16)
    real_hgrad = (conv_back(real_cot, second) * leak_slope(real_hidden)).astype(BF16)
    input_grad = x_grad(real, real_cot, real_hgrad)
    sample_hgrad = -((chain_inner * leak_slope(sample_hidden)).astype(BF16))

    def bias_sum(values):
        return jnp.sum(values.astype(F32), axis=(0, 1, 2))

    totals = (
        kernel_partial(real_lower, real_hgrad) + kernel_partial(sample_lower, sample_hgrad),
        bias_sum(real_hgrad) + bias_sum(sample_hgrad),
        kernel_partial(real_upper, real_cot) + kernel_partial(sample_upper, -chain_cot),
        bias_sum(real_cot) - bias_sum(chain_cot),
    )
    channels = kernel_one.shape[3]
    kernel_shape = (3, 3, channels, channels)
    shares = (
        lax.psum_scatter(totals[0].reshape(kernel_shape), "wide", scatter_dimension=2, tiled=True),
        lax.psum_scatter(totals[1], "wide", scatter_dimension=0, tiled=True),
        lax.psum_scatter(totals[2].reshape(kernel_shape), "wide", scatter_dimension=2, tiled=True),
        lax.psum_scatter(totals[3], "wide", scatter_dimension=0, tiled=True),
    )
    summed = lax.psum(shares, "dp")
    return (block_output, input_grad, state, summed[0], summed[1], summed[2], summed[3])


NW = 8
C = 640
CS = C // NW
PX = 768
RS = 9 * CS
GR = 3 * CS
LT = 128
TAPS = [(p - 1, q - 1) for p in range(3) for q in range(3)]

PB_CS = 2 * RS
PB_XS = PB_CS + 4 * 2 * GR
PB_YS = PB_XS + 4 * GR
PB_ZS = PB_YS + 2 * GR
PB_FS = PB_ZS + 2 * GR
OWN_ROW = 4 * GR

RIGHT, LEFT, YN, SIB, XN = range(5)


def tn(a, b):
    return lax.dot_general(a, b, (((0,), (0,)), ((), ())), preferred_element_type=F32)


def nt(a, b):
    return lax.dot_general(a, b, (((1,), (1,)), ((), ())), preferred_element_type=F32)


def nn(a, b):
    return jnp.dot(a, b, preferred_element_type=F32)


def leak(v):
    return jnp.where(v > 0, v, 0.2 * v)


def slope(v):
    return jnp.where(v > 0, 1.0, 0.2).astype(F32)


def inside(di, dj):
    lane = lax.broadcasted_iota(jnp.int32, (1, LT), 1)
    row, col = (lane // 8) % 8 + di, lane % 8 + dj
    return (row >= 0) & (row < 8) & (col >= 0) & (col < 8)


def turn(v, by):
    by %= LT
    return v if by == 0 else pltpu.roll(v, by, 1)


def moved(v, di, dj):
    if di == 0 and dj == 0:
        return v
    return jnp.where(inside(di, dj), turn(v, -(8 * di + dj)), jnp.zeros_like(v))


def al(row, by=16):
    return pl.multiple_of(row, by)


def body(
    xr, xc, nz, gr, gc, k1, k2, bt,
    o_blk, o_ig, o_fs, o_g1, o_g2, o_b,
    W, XIN, GT, NT, XRT, L, SI, H, HG, UP, PB, SP, G, OUT, BC, BT, BG,
    CR, XRV, YR, FXR, FCR,
    in_sem, own_sem, out_sem, b_ssem, b_rsem, g_ssem, g_rsem,
    cs_sem, cr_sem, xs_sem, xr_sem, ys_sem, yr_sem, zs_sem, zr_sem, fs_sem, fr_sem, f2s_sem, f2r_sem,
    bgs_sem, bgr_sem,
):
    dp, w = lax.axis_index("dp"), lax.axis_index("wide")
    x, c = lax.div(dp, 2), lax.rem(dp, 2)
    z, y = lax.div(w, 2), lax.rem(w, 2)
    d_sib = (x * 2 + 1 - c, w)
    d_x = ((1 - x) * 2 + c, w)
    d_y = (dp, z * 2 + 1 - y)
    d_right = (dp, w + 2)
    d_left = (dp, w - 2)
    own_g = c * (1 + x)
    oth_g = c * (2 - x)

    def ring_z(by):
        return lax.rem(z + by, 4)

    barrier = pltpu.get_barrier_semaphore()
    greeted = [d_sib, d_x] + [(dp, lax.rem(w + by, NW)) for by in range(1, NW)]
    for dev in greeted:
        pl.semaphore_signal(barrier, inc=1, device_id=dev, device_id_type=MESH)

    def own_copy(k):
        return pltpu.make_async_copy((k1, k2)[k], W.at[k * NW + w], own_sem.at[k])

    own_copy(0).start()
    own_copy(1).start()
    bt_copy = pltpu.make_async_copy(bt, BT.at[w], own_sem.at[2])
    bt_copy.start()
    sources = [xc, xr, gc, gr, nz.at[0], nz.at[1]]

    def in_copy(n):
        return pltpu.make_async_copy(sources[n], XIN.at[n % 2], in_sem.at[n % 2])

    in_copy(0).start()
    in_copy(1).start()
    own_copy(0).wait()
    own_copy(1).wait()
    bt_copy.wait()
    pl.semaphore_wait(barrier, len(greeted))

    devs = {RIGHT: d_right, LEFT: d_left, YN: d_y, SIB: d_sib, XN: d_x}

    def message(k, s, tap, way):
        part = W.at[k * NW + s, pl.ds(al(tap * CS), CS), :]
        return pltpu.make_async_remote_copy(
            src_ref=part, dst_ref=part, send_sem=g_ssem.at[way], recv_sem=g_rsem.at[k, s, tap],
            device_id=devs[way], device_id_type=MESH,
        )

    def arrive(k, s, tap):
        message(k, s, tap, YN).wait_recv()

    def events(k, m):
        def z_part(n, j):
            tap = own_g * 3 + j

            @pl.when(n == 0)
            def _():
                @pl.when(z < 3)
                def _():
                    message(k, w, tap, RIGHT).start()

                @pl.when(z > 0)
                def _():
                    message(k, w, tap, LEFT).start()

                message(k, w, tap, YN).start()

            def flow(zz, onward, may):
                s = zz * 2 + y
                arrive(k, s, tap)

                @pl.when(may)
                def _():
                    message(k, s, tap, onward).start()

                message(k, s, tap, YN).start()
                message(k, s, tap, SIB).start()

                @pl.when(c == 1)
                def _():
                    message(k, s, tap, XN).start()

            @pl.when((n >= 1) & (z - n >= 0))
            def _():
                flow(z - n, RIGHT, z < 3)

            @pl.when((n >= 1) & (z + n <= 3))
            def _():
                flow(z + n, LEFT, z > 0)

        def y_part(n, j):
            tap = own_g * 3 + j

            def flow(zz):
                s = zz * 2 + 1 - y
                arrive(k, s, tap)
                message(k, s, tap, SIB).start()

                @pl.when(c == 1)
                def _():
                    message(k, s, tap, XN).start()

            @pl.when(z - n >= 0)
            def _():
                flow(z - n)

            @pl.when((n >= 1) & (z + n <= 3))
            def _():
                flow(z + n)

        def x_part(n, j, yy, least):
            tap = oth_g * 3 + j

            def flow(zz):
                s = zz * 2 + yy
                arrive(k, s, tap)
                message(k, s, tap, SIB).start()

            @pl.when((c == 1) & (n >= least) & (z - n >= 0))
            def _():
                flow(z - n)

            @pl.when((c == 1) & (n >= 1) & (z + n <= 3))
            def _():
                flow(z + n)

        for lag, part in (
            (2, lambda n, j: x_part(n, j, 1 - y, 0)),
            (1, lambda n, j: x_part(n, j, y, 1)),
            (1, y_part),
            (0, z_part),
        ):
            at = m - lag

            @pl.when((at >= 0) & (at < 12))
            def _(part=part, at=at):
                at = jnp.maximum(at, 0)
                part(lax.div(at, 3), lax.rem(at, 3))

    def ready(k, s):
        @pl.when(s != w)
        def _():
            @pl.when(c == 0)
            def _():
                for tap in range(3, 9):
                    arrive(k, s, tap)

            @pl.when(c == 1)
            def _():
                for tap in range(3):
                    arrive(k, s, tap)

    def bias_message(by):
        return pltpu.make_async_remote_copy(
            src_ref=BT.at[w], dst_ref=BT.at[w], send_sem=b_ssem.at[by], recv_sem=b_rsem.at[w],
            device_id=(dp, lax.rem(w + by, NW)), device_id_type=MESH,
        )

    def bias_arrive(by):
        s = lax.rem(w + by, NW)
        pltpu.make_async_remote_copy(
            src_ref=BT.at[s], dst_ref=BT.at[s], send_sem=b_ssem.at[by], recv_sem=b_rsem.at[s],
            device_id=(dp, s), device_id_type=MESH,
        ).wait_recv()

    events(0, 0)
    for by in range(1, NW):
        bias_message(by).start()

    S0, I0 = 0, C

    for n in range(6):
        in_copy(n).wait()
        if n == 0:
            t = XIN[0].T.astype(F32)
            SI[S0 : S0 + C, :] = t
            L[0] = leak(t).astype(BF16)
        elif n == 1:
            t = XIN[1].T
            XRT[...] = t
            L[1] = leak(t.astype(F32)).astype(BF16)
        elif n < 4:
            GT[n - 2] = XIN[n % 2].T
        else:
            NT[n - 4] = XIN[n % 2].T
        if n + 2 < 6:
            in_copy(n + 2).start()
        events(0, n + 1) if n < 2 else None
    H[...] = jnp.zeros_like(H)
    events(0, 3)
    for by in range(1, NW):
        bias_arrive(by)

    def bias_columns(s, carry):
        for k in range(2):
            row = jnp.broadcast_to(BT[s, k : k + 1, :], (LT, LT))
            BC[k, pl.ds(al(s * CS), CS), :] = row.T[0:CS, :]
        return carry

    lax.fori_loop(0, NW, bias_columns, 0)

    def rows_of(s):
        return pl.ds(al(s * CS), CS)

    def cols(n):
        return slice(n * LT, (n + 1) * LT)

    def patches(load, row):
        for n in range(PX // LT):
            v = load(cols(n))
            for t, (di, dj) in enumerate(TAPS):
                PB[pl.ds(al(row + t * CS), CS), cols(n)] = moved(v, di, dj)

    def spread_back(k, s, cot, use):
        for n in range(PX // 256):
            SP[...] = nn(W[k * NW + s], cot[:, n * 256 : (n + 1) * 256])
            for h in range(2):
                total = None
                for t, (di, dj) in enumerate(TAPS):
                    v = moved(SP[t * CS : (t + 1) * CS, h * LT : (h + 1) * LT], -di, -dj)
                    total = v if total is None else total + v
                use(cols(2 * n + h), total)

    def take_first(s):
        ready(0, s)
        for part in range(2):
            patches(lambda at: L[part, rows_of(s), at], part * RS)
            H[part] += tn(W[s], PB[part * RS : (part + 1) * RS, :])

    def take_second(s):
        ready(1, s)

        def chain(at, inner):
            hid = H[0, rows_of(s), at] + BC[0, rows_of(s), :]
            SI[pl.ds(al(I0 + s * CS), CS), at] = inner
            HG[0, rows_of(s), at] = (inner * slope(hid)).astype(BF16)

        spread_back(1, s, GT.at[0], chain)

        def real(at, inner):
            hid = H[1, rows_of(s), at] + BC[0, rows_of(s), :]
            HG[1, rows_of(s), at] = (inner * slope(hid)).astype(BF16)
            UP[1, rows_of(s), at] = leak(hid).astype(BF16)

        spread_back(1, s, GT.at[1], real)

    def turns(q, take):
        @pl.when((q >= 0) & (q < 12))
        def _():
            n, part = lax.div(jnp.maximum(q, 0), 3), lax.rem(jnp.maximum(q, 0), 3)

            def one(u, carry):
                side, flip = lax.rem(u, 2), lax.div(u, 2)
                zz = z + (2 * side - 1) * n
                yy = y + flip - 2 * y * flip

                @pl.when((zz >= 0) & (zz <= 3) & ((n > 0) | (side == 0)))
                def _():
                    take(zz * 2 + yy)

                return carry

            lax.fori_loop(part, part + 1 + lax.div(part, 2), one, 0)

    def slot(r, carry):
        events(0, r)
        events(1, r - 12)
        turns(r - 5, take_first)
        turns(r - 17, take_second)
        return carry

    lax.fori_loop(4, 29, slot, 0)

    def whole_first():
        def build(s, carry):
            patches(lambda at: L[0, rows_of(s), at], s * RS)
            return carry

        lax.fori_loop(0, NW, build, 0)

        def product(n, carry):
            at = pl.ds(al(n * 256, 256), 256)
            H[0, :, at] = tn(W[0:NW].reshape(NW * RS, C), PB[:, at])
            return carry

        lax.fori_loop(0, PX // 256, product, 0)

    def whole_back():
        def build(s, carry):
            for n in range(PX // LT):
                v = HG[0, rows_of(s), cols(n)]
                for t, (di, dj) in enumerate(TAPS):
                    PB[pl.ds(al(t * C + s * CS), CS), cols(n)] = moved(v, -di, -dj)
            return carry

        lax.fori_loop(0, NW, build, 0)

        def product(n, carry):
            at = pl.ds(al(n * 256, 256), 256)
            left = jnp.concatenate(
                [
                    jnp.concatenate([W[s, t * CS : (t + 1) * CS, :] for s in range(NW)], axis=0)
                    for t in range(9)
                ],
                axis=1,
            )
            H[0, :, at] = nn(left, PB[:, at])
            return carry

        lax.fori_loop(0, PX // 256, product, 0)

    def step_state(k):
        def one(s, carry):
            for n in range(PX // LT):
                state = SI[pl.ds(al(S0 + s * CS), CS), cols(n)]
                pull = GT[0, rows_of(s), cols(n)].astype(F32) + slope(state) * H[0, rows_of(s), cols(n)]
                state = state - pull + 0.01 * NT[k, rows_of(s), cols(n)].astype(F32)
                SI[pl.ds(al(S0 + s * CS), CS), cols(n)] = state
                L[0, rows_of(s), cols(n)] = leak(state).astype(BF16)
            return carry

        lax.fori_loop(0, NW, one, 0)

    def hidden_grads(last):
        def one(s, carry):
            for n in range(PX // LT):
                hid = H[0, rows_of(s), cols(n)] + BC[0, rows_of(s), :]
                grad = (SI[pl.ds(al(I0 + s * CS), CS), cols(n)] * slope(hid)).astype(BF16)
                if last:
                    HG[0, rows_of(s), cols(n)] = -grad
                    UP[0, rows_of(s), cols(n)] = leak(hid).astype(BF16)
                    GT[0, rows_of(s), cols(n)] = -GT[0, rows_of(s), cols(n)]
                else:
                    HG[0, rows_of(s), cols(n)] = grad
            return carry

        lax.fori_loop(0, NW, one, 0)

    whole_back()
    step_state(0)
    whole_first()
    hidden_grads(False)
    whole_back()
    step_state(1)
    OUT[...] = SI[S0 : S0 + C, :].T

    def out_copy(ref, rows=PX):
        return pltpu.make_async_copy(OUT.at[0:rows], ref, out_sem)

    out_copy(o_fs).start()
    whole_first()
    hidden_grads(True)

    ones = jnp.ones((8, PX), BF16)
    BG[0, 0:8, :] = nt(ones, HG[0]) + nt(ones, HG[1])
    BG[0, 8:16, :] = nt(ones, GT[0]) + nt(ones, GT[1])

    def bg_send(src, dst, sem, dev):
        return pltpu.make_async_remote_copy(
            src_ref=BG.at[src], dst_ref=BG.at[dst], send_sem=bgs_sem.at[sem], recv_sem=bgr_sem.at[sem],
            device_id=dev, device_id_type=MESH,
        )

    def bg_step(i):
        @pl.when(i == 1)
        def _():
            bg_send(0, 3, 0, d_sib).start()

        @pl.when(i == 2)
        def _():
            bg_send(0, 3, 0, d_sib).wait()
            BG[1] = BG[0] + BG[3]
            bg_send(1, 4, 1, d_x).start()

        @pl.when(i == 4)
        def _():
            bg_send(1, 4, 1, d_x).wait()
            BG[2] = BG[1] + BG[4]
            bg_send(2, 5, 2, d_y).start()

        @pl.when(i == 6)
        def _():
            bg_send(2, 5, 2, d_y).wait()
            BG[6 + z] = BG[2] + BG[5]
            for by in range(1, 4):
                bg_send(6 + z, 6 + z, 2 + by, (dp, ring_z(by) * 2 + y)).start()

        @pl.when(i == 9)
        def _():
            for by in range(1, 4):
                bg_send(6 + z, 6 + z, 2 + by, (dp, ring_z(by) * 2 + y)).wait()
            BG[0] = BG[6] + BG[7] + BG[8] + BG[9]
            pltpu.make_async_copy(BG.at[0], o_b, own_sem.at[3]).start()

    def shard_of(a):
        p = lax.rem(a, 8)
        zz = ring_z(1 + lax.div(p, 2))
        yy = lax.rem(y + 1 + lax.rem(p, 2), 2)
        return zz, yy

    def first_block(s, buf):
        for part in range(2):
            patches(lambda at: L[part, rows_of(s), at], part * RS)
        G[buf] = nt(PB[0:RS, :], HG[0]) + nt(PB[RS : 2 * RS, :], HG[1])

        def keep(at, total):
            H[0, rows_of(s), at] = total

        spread_back(0, s, HG.at[1], keep)

    def second_block(s, buf, start):
        for part in range(2):
            patches(lambda at: UP[part, rows_of(s), at], part * RS)
        G[buf] = nt(PB[0:RS, :], GT[0]) + nt(PB[RS : 2 * RS, :], GT[1])
        add = tn(W[NW + s], PB[RS : 2 * RS, :])

        @pl.when(start)
        def _():
            H[1] = add

        @pl.when(jnp.logical_not(start))
        def _():
            H[1] += add

    def remote(src, dst, ss, rs, dev):
        return pltpu.make_async_remote_copy(
            src_ref=src, dst_ref=dst, send_sem=ss, recv_sem=rs, device_id=dev, device_id_type=MESH
        )

    def core_send(a, core):
        q = lax.rem(a, 4)
        rows = 2 * GR if core == 0 else GR
        return remote(
            PB.at[pl.ds(al(PB_CS + q * 2 * GR), rows), 0:C], CR.at[q, 0:rows], cs_sem.at[q], cr_sem.at[q], d_sib
        )

    def x_send(a):
        q = lax.rem(a, 4)
        return remote(PB.at[pl.ds(al(PB_XS + q * GR), GR), 0:C], XRV.at[q], xs_sem.at[q], xr_sem.at[q], d_x)

    def y_send(a, zz):
        q = lax.rem(lax.div(a, 2), 2)
        at = lax.div(a, 8) * 4 + zz
        return remote(PB.at[pl.ds(al(PB_YS + q * GR), GR), 0:C], YR.at[at], ys_sem.at[q], yr_sem.at[at], d_y)

    def z_send(a, by):
        q = lax.rem(lax.div(a, 2), 2)
        at = lax.div(a, 8) * 3 + by - 1
        land = XIN.at[lax.div(a, 8), pl.ds(al((by - 1) * GR), GR), :]
        return remote(
            PB.at[pl.ds(al(PB_ZS + q * GR), GR), 0:C], land, zs_sem.at[q], zr_sem.at[at], (dp, ring_z(by) * 2 + y)
        )

    def f_rows(turn_):
        return pl.ds(PB_FS + turn_ * GR, GR)

    def f_send(turn_):
        return remote(PB.at[f_rows(turn_), 0:C], FXR.at[turn_], fs_sem.at[turn_], fr_sem.at[turn_], d_x)

    def f2_own(turn_, core):
        to = FCR.at[turn_, 0:GR] if core == 0 else FCR.at[turn_, pl.ds(al((own_g - 1) * GR), GR)]
        return remote(PB.at[f_rows(turn_), 0:C], to, f2s_sem.at[turn_, 0], f2r_sem.at[turn_, 0], d_sib)

    def f2_oth(turn_):
        to = FCR.at[turn_, pl.ds(al((oth_g - 1) * GR), GR)]
        return remote(FXR.at[turn_], to, f2s_sem.at[turn_, 1], f2r_sem.at[turn_, 1], d_sib)

    def acc(a):
        return pl.ds(al(lax.rem(a, 4) * GR), GR)

    def reduce_step(i, carry):
        @pl.when(i < 16)
        def _():
            zz, yy = shard_of(i)
            s = zz * 2 + yy
            buf = lax.rem(i, 2)

            @pl.when(i < 8)
            def _():
                second_block(s, buf, i == 0)

            @pl.when(i >= 8)
            def _():
                first_block(s, buf)

            q = lax.rem(i, 4)
            base = PB_CS + q * 2 * GR

            @pl.when(c == 0)
            def _():
                @pl.when(i >= 4)
                def _():
                    core_send(i - 4, 0).wait_send()

                PB[pl.ds(al(base), 2 * GR), 0:C] = G[buf, GR : 3 * GR, :].astype(BF16)
                core_send(i, 0).start()

            @pl.when(c == 1)
            def _():
                @pl.when(i >= 4)
                def _():
                    core_send(i - 4, 1).wait_send()

                PB[pl.ds(al(base), GR), 0:C] = G[buf, 0:GR, :].astype(BF16)
                core_send(i, 1).start()

        @pl.when((i >= 1) & (i < 17))
        def _():
            a = i - 1
            q, buf = lax.rem(a, 4), lax.rem(a, 2)

            @pl.when(c == 0)
            def _():
                core_send(a, 1).wait_recv()
                SI[acc(a), 0:C] = G[buf, 0:GR, :] + CR[q, 0:GR, :].astype(F32)

            @pl.when(c == 1)
            def _():
                core_send(a, 0).wait_recv()

                @pl.when(a >= 4)
                def _():
                    x_send(a - 4).wait_send()

                PB[pl.ds(al(PB_XS + q * GR), GR), 0:C] = (
                    G[buf, pl.ds(al(oth_g * GR), GR), :]
                    + CR[q, pl.ds(al(jnp.maximum(oth_g - 1, 0) * GR), GR), :].astype(F32)
                ).astype(BF16)
                x_send(a).start()
                SI[acc(a), 0:C] = (
                    G[buf, pl.ds(al(own_g * GR), GR), :]
                    + CR[q, pl.ds(al(jnp.maximum(own_g - 1, 0) * GR), GR), :].astype(F32)
                )

        @pl.when((i >= 2) & (i < 18))
        def _():
            a = i - 2
            zz, yy = shard_of(a)

            @pl.when(c == 1)
            def _():
                x_send(a).wait_recv()
                SI[acc(a), 0:C] += XRV[lax.rem(a, 4)].astype(F32)

            @pl.when(lax.rem(a, 2) == 0)
            def _():
                @pl.when(a >= 4)
                def _():
                    y_send(a - 4, 0).wait_send()

                q = lax.rem(lax.div(a, 2), 2)
                PB[pl.ds(al(PB_YS + q * GR), GR), 0:C] = SI[acc(a), 0:C].astype(BF16)
                y_send(a, zz).start()

        @pl.when((i >= 5) & (i < 20) & (lax.rem(i, 2) == 1))
        def _():
            a = i - 4
            zz, yy = shard_of(a)
            y_send(a, zz).wait_recv()
            total = SI[acc(a), 0:C] + YR[lax.div(a, 8) * 4 + zz].astype(F32)
            pair = lax.div(lax.rem(a, 8), 2)
            q = lax.rem(lax.div(a, 2), 2)

            @pl.when(pair < 3)
            def _():
                @pl.when(a >= 5)
                def _():
                    z_send(a, 1).wait_send()

                PB[pl.ds(al(PB_ZS + q * GR), GR), 0:C] = total.astype(BF16)
                for by in range(1, 4):

                    @pl.when(pair == by - 1)
                    def _(by=by):
                        z_send(a, by).start()

            @pl.when(pair == 3)
            def _():
                SI[OWN_ROW : OWN_ROW + GR, 0:C] = total

        for turn_, ref in ((0, o_g2), (1, o_g1)):
            base = 8 * turn_

            @pl.when(i == base + 12)
            def _(turn_=turn_, base=base):
                total = SI[OWN_ROW : OWN_ROW + GR, 0:C]
                for by in range(1, 4):
                    z_send(base, by).wait_recv()
                    total = total + XIN[turn_, (by - 1) * GR : by * GR, :].astype(F32)
                PB[f_rows(turn_), 0:C] = total.astype(BF16)
                f_send(turn_).start()

            @pl.when(i == base + 14)
            def _(turn_=turn_):
                f_send(turn_).wait()

                @pl.when(c == 0)
                def _():
                    both = PB[f_rows(turn_), 0:C].astype(F32) + FXR[turn_].astype(F32)
                    PB[f_rows(turn_), 0:C] = both.astype(BF16)
                    f2_own(turn_, 0).start()

                @pl.when(c == 1)
                def _():
                    f2_own(turn_, 1).start()
                    f2_oth(turn_).start()

            @pl.when(i == base + 15)
            def _(turn_=turn_, ref=ref):
                out_copy(o_fs).wait()

                @pl.when(c == 0)
                def _():
                    f2_own(turn_, 0).wait_send()
                    for part in range(2):
                        got = FCR.at[turn_, part * GR : (part + 1) * GR]
                        remote(got, got, f2s_sem.at[turn_, part], f2r_sem.at[turn_, part], d_sib).wait_recv()
                    OUT[0:GR, :] = PB[f_rows(turn_), 0:C].astype(F32)
                    OUT[GR : 3 * GR, :] = FCR[turn_].astype(F32)

                @pl.when(c == 1)
                def _():
                    f2_own(turn_, 1).wait_send()
                    f2_oth(turn_).wait_send()
                    f2_own(turn_, 0).wait_recv()
                    OUT[0:GR, :] = FCR[turn_, 0:GR].astype(F32)
                    OUT[pl.ds(al(jnp.maximum(own_g, 1) * GR), GR), :] = PB[f_rows(turn_), 0:C].astype(F32)
                    OUT[pl.ds(al(jnp.maximum(oth_g, 1) * GR), GR), :] = FXR[turn_].astype(F32)

                out_copy(ref, RS).start()

        @pl.when(i == 8)
        def _():
            out_copy(o_fs).wait()
            for n in range(PX // LT):
                whole = XRT[:, cols(n)].astype(F32) + H[1, :, cols(n)] + BC[1]
                OUT[n * LT : (n + 1) * LT, :] = whole.T
            out_copy(o_blk).start()

        @pl.when(i == 16)
        def _():
            out_copy(o_g2, RS).wait()
            for n in range(PX // LT):
                whole = GT[1, :, cols(n)].astype(F32) + slope(XRT[:, cols(n)].astype(F32)) * H[0, :, cols(n)]
                OUT[n * LT : (n + 1) * LT, :] = whole.T
            out_copy(o_ig).start()

        bg_step(i)
        return carry

    lax.fori_loop(0, 24, reduce_step, 0)

    out_copy(o_g1, RS).wait()
    pltpu.make_async_copy(BG.at[0], o_b, own_sem.at[3]).wait()
    for by in range(1, NW):
        bias_message(by).wait_send()

    def drain(way, planes, rows):
        part = W.at[0:planes, 0:rows, :]
        remote(part, part, g_ssem.at[way], g_rsem.at[0, 0, 0], d_sib).wait_send()

    for zz in range(4):

        @pl.when(z == zz)
        def _(zz=zz):
            if zz < 3:
                drain(RIGHT, 2 * (zz + 1), GR)
            if zz > 0:
                drain(LEFT, 2 * (4 - zz), GR)

    drain(YN, 8, GR)

    @pl.when(c == 0)
    def _():
        drain(SIB, 14, GR)
        for a in range(12, 16):
            core_send(a, 0).wait_send()

    @pl.when(c == 1)
    def _():
        drain(SIB, 14, 2 * GR)
        drain(XN, 14, GR)
        for a in range(12, 16):
            core_send(a, 1).wait_send()
            x_send(a).wait_send()

    for a in (12, 14):
        y_send(a, 0).wait_send()
    z_send(11, 1).wait_send()
    z_send(13, 1).wait_send()


def kernel_local(real_images, replay_chains, langevin_noise, real_cot, chain_cot, kernel_one, bias_one, kernel_two, bias_two):
    def flat(values):
        return values.reshape(values.shape[:-4] + (PX, C))

    rows = jnp.stack([bias_one, bias_two]).astype(F32)
    bias_tile = jnp.pad(rows, ((0, 6), (0, LT - CS)))
    anywhere = pl.BlockSpec(memory_space=pl.ANY)
    dma = pltpu.SemaphoreType.DMA
    out_shape = [jax.ShapeDtypeStruct((PX, C), F32)] * 3 + [jax.ShapeDtypeStruct((RS, C), F32)] * 2
    out_shape += [jax.ShapeDtypeStruct((16, C), F32)]
    scratch = [
        pltpu.VMEM((2 * NW, RS, C), BF16),
        pltpu.VMEM((2, PX, C), BF16),
        pltpu.VMEM((2, C, PX), BF16),
        pltpu.VMEM((2, C, PX), BF16),
        pltpu.VMEM((C, PX), BF16),
        pltpu.VMEM((2, C, PX), BF16),
        pltpu.VMEM((2 * C, PX), F32),
        pltpu.VMEM((2, C, PX), F32),
        pltpu.VMEM((2, C, PX), BF16),
        pltpu.VMEM((2, C, PX), BF16),
        pltpu.VMEM((NW * RS, PX), BF16),
        pltpu.VMEM((RS, 256), F32),
        pltpu.VMEM((2, RS, C), F32),
        pltpu.VMEM((PX, C), F32),
        pltpu.VMEM((2, C, LT), F32),
        pltpu.VMEM((NW, 8, LT), F32),
        pltpu.VMEM((10, 16, C), F32),
        pltpu.VMEM((4, 2 * GR, C), BF16),
        pltpu.VMEM((4, GR, C), BF16),
        pltpu.VMEM((8, GR, C), BF16),
        pltpu.VMEM((2, GR, C), BF16),
        pltpu.VMEM((2, 2 * GR, C), BF16),
        dma((2,)), dma((4,)), dma, dma((NW,)), dma((NW,)), dma((5,)), dma((2, NW, 9)),
        dma((4,)), dma((4,)), dma((4,)), dma((4,)), dma((2,)), dma((8,)), dma((2,)), dma((6,)),
        dma((2,)), dma((2,)), dma((2, 2)), dma((2, 2)), dma((6,)), dma((6,)),
    ]
    blk, ig, fs, g1, g2, bsum = pl.pallas_call(
        body,
        out_shape=out_shape,
        in_specs=[anywhere] * 8,
        out_specs=[anywhere] * 6,
        scratch_shapes=scratch,
        compiler_params=pltpu.CompilerParams(
            collective_id=0, has_side_effects=True, vmem_limit_bytes=63 * 2**20
        ),
    )(
        flat(real_images), flat(replay_chains), flat(langevin_noise), flat(real_cot), flat(chain_cot),
        kernel_one.reshape(RS, C), kernel_two.reshape(RS, C), bias_tile,
    )
    at = lax.axis_index("wide") * CS
    shape = real_images.shape
    return (
        blk.reshape(shape), ig.reshape(shape), fs.reshape(shape),
        g1.reshape(kernel_one.shape), lax.dynamic_slice(bsum[0], (at,), (CS,)),
        g2.reshape(kernel_two.shape), lax.dynamic_slice(bsum[8], (at,), (CS,)),
    )


def solution(mesh):
    def local(real_images, *rest):
        kernel_one = rest[4]
        fits = (
            mesh.shape["dp"] == 4
            and mesh.shape["wide"] == NW
            and real_images.shape == (12, 8, 8, C)
            and kernel_one.shape == (3, 3, CS, C)
            and rest[1].shape[0] == 2
        )
        return (kernel_local if fits else plain_local)(real_images, *rest)

    return jax.shard_map(
        local,
        mesh=mesh,
        in_specs=(
            P(("dp", "wide"), None, None, None),
            P(("dp", "wide"), None, None, None),
            P(None, ("dp", "wide"), None, None, None),
            P(("dp", "wide"), None, None, None),
            P(("dp", "wide"), None, None, None),
            P(None, None, "wide", None),
            P("wide"),
            P(None, None, "wide", None),
            P("wide"),
        ),
        out_specs=(
            P(("dp", "wide"), None, None, None),
            P(("dp", "wide"), None, None, None),
            P(("dp", "wide"), None, None, None),
            P(None, None, "wide", None),
            P("wide"),
            P(None, None, "wide", None),
            P("wide"),
        ),
        check_vma=False,
    )
```

```python
import functools

import jax
import jax.numpy as jnp
from jax import lax
from jax.experimental import pallas as pl
from jax.experimental.pallas import tpu as pltpu
from jax.sharding import PartitionSpec as P

F32 = jnp.float32
BF16 = jnp.bfloat16
MESH = pl.DeviceIdType.MESH


def leaky_relu(values):
    return jnp.where(values > 0, values, 0.2 * values)


def leak_slope(values):
    return jnp.where(values > 0, 1.0, 0.2).astype(F32)


def tap_patches(activation):
    batch_size, height, map_width, channels = activation.shape
    padded = jnp.pad(activation, ((0, 0), (1, 1), (1, 1), (0, 0)))
    tap_list = [
        padded[:, row_off : row_off + height, col_off : col_off + map_width, :]
        for row_off in range(3)
        for col_off in range(3)
    ]
    return jnp.stack(tap_list, axis=3).reshape(batch_size * height * map_width, 9 * channels)


def conv_apply(activation, kernel_mat, bias_row):
    result = jnp.dot(tap_patches(activation), kernel_mat, preferred_element_type=F32)
    return result.reshape(activation.shape[:3] + (kernel_mat.shape[1],)) + bias_row.astype(F32)


def conv_back(gradient, kernel_mat):
    batch_size, height, map_width, channels = gradient.shape
    in_channels = kernel_mat.shape[0] // 9
    spread = lax.dot_general(
        gradient.reshape(-1, channels), kernel_mat, (((1,), (1,)), ((), ())), preferred_element_type=F32
    )
    spread = spread.reshape(batch_size, height, map_width, 9, in_channels)
    summed = jnp.zeros((batch_size, height + 2, map_width + 2, in_channels), F32)
    for row_off in range(3):
        for col_off in range(3):
            summed = summed + jnp.pad(
                spread[:, :, :, 3 * row_off + col_off, :],
                ((0, 0), (row_off, 2 - row_off), (col_off, 2 - col_off), (0, 0)),
            )
    return summed[:, 1 : height + 1, 1 : map_width + 1, :]


def kernel_partial(activation, gradient):
    channels = gradient.shape[3]
    return lax.dot_general(
        tap_patches(activation),
        gradient.reshape(-1, channels),
        (((0,), (0,)), ((), ())),
        preferred_element_type=F32,
    )


def plain_local(real_images, replay_chains, langevin_noise, real_cot, chain_cot, kernel_one, bias_one, kernel_two, bias_two):
    def whole(kernel):
        gathered = lax.all_gather(kernel, "wide", axis=2, tiled=True)
        return gathered.reshape(9 * gathered.shape[2], gathered.shape[3])

    first, second = whole(kernel_one), whole(kernel_two)
    first_bias = lax.all_gather(bias_one, "wide", axis=0, tiled=True)
    second_bias = lax.all_gather(bias_two, "wide", axis=0, tiled=True)

    def hidden_of(values):
        lower = leaky_relu(values).astype(BF16)
        return lower, conv_apply(lower, first, first_bias)

    def x_grad(values, cot, hidden_grad):
        return cot.astype(F32) + leak_slope(values) * conv_back(hidden_grad, first)

    chain_inner = conv_back(chain_cot, second)
    state = replay_chains.astype(F32)
    for step_index in range(langevin_noise.shape[0]):
        _, hidden = hidden_of(state)
        hidden_grad = (chain_inner * leak_slope(hidden)).astype(BF16)
        state = state - x_grad(state, chain_cot, hidden_grad) + 0.01 * langevin_noise[step_index].astype(F32)
    real = real_images.astype(F32)
    real_lower, real_hidden = hidden_of(real)
    real_upper = leaky_relu(real_hidden).astype(BF16)
    block_output = real + conv_apply(real_upper, second, second_bias)
    sample_lower, sample_hidden = hidden_of(state)
    sample_upper = leaky_relu(sample_hidden).astype(BF16)
    real_hgrad = (conv_back(real_cot, second) * leak_slope(real_hidden)).astype(BF16)
    input_grad = x_grad(real, real_cot, real_hgrad)
    sample_hgrad = -((chain_inner * leak_slope(sample_hidden)).astype(BF16))

    def bias_sum(values):
        return jnp.sum(values.astype(F32), axis=(0, 1, 2))

    totals = (
        kernel_partial(real_lower, real_hgrad) + kernel_partial(sample_lower, sample_hgrad),
        bias_sum(real_hgrad) + bias_sum(sample_hgrad),
        kernel_partial(real_upper, real_cot) + kernel_partial(sample_upper, -chain_cot),
        bias_sum(real_cot) - bias_sum(chain_cot),
    )
    channels = kernel_one.shape[3]
    kernel_shape = (3, 3, channels, channels)
    shares = (
        lax.psum_scatter(totals[0].reshape(kernel_shape), "wide", scatter_dimension=2, tiled=True),
        lax.psum_scatter(totals[1], "wide", scatter_dimension=0, tiled=True),
        lax.psum_scatter(totals[2].reshape(kernel_shape), "wide", scatter_dimension=2, tiled=True),
        lax.psum_scatter(totals[3], "wide", scatter_dimension=0, tiled=True),
    )
    summed = lax.psum(shares, "dp")
    return (block_output, input_grad, state, summed[0], summed[1], summed[2], summed[3])


NW = 8
C = 640
CS = C // NW
PX = 768
RS = 9 * CS
GR = 3 * CS
LT = 128
TAPS = [(p - 1, q - 1) for p in range(3) for q in range(3)]

LAG_C, LAG_D = 2, 4
XSLOTS = 2 * LAG_C
F2 = 8 + LAG_D
F3 = F2 + 1

RIGHT, LEFT, YN, SIB, XN = range(5)
LAG_Y, LAG_X = 3, 3
LAG_T = max(LAG_X, LAG_Y + LAG_X - 1) + 3


def tn(a, b):
    return lax.dot_general(a, b, (((0,), (0,)), ((), ())), preferred_element_type=F32)


def nt(a, b):
    return lax.dot_general(a, b, (((1,), (1,)), ((), ())), preferred_element_type=F32)


def nn(a, b):
    return jnp.dot(a, b, preferred_element_type=F32)


def leak(v):
    return jnp.where(v > 0, v, 0.2 * v)


def slope(v):
    return jnp.where(v > 0, 1.0, 0.2).astype(F32)


def inside(di, dj):
    lane = lax.broadcasted_iota(jnp.int32, (1, LT), 1)
    row, col = (lane // 8) % 8 + di, lane % 8 + dj
    return (row >= 0) & (row < 8) & (col >= 0) & (col < 8)


def turn(v, by):
    by %= LT
    return v if by == 0 else pltpu.roll(v, by, 1)


def moved(v, di, dj):
    if di == 0 and dj == 0:
        return v
    return jnp.where(inside(di, dj), turn(v, -(8 * di + dj)), jnp.zeros_like(v))


def al(row, by=16):
    return pl.multiple_of(row, by)


def body(
    xr, xc, nz, gr, gc, k1, k2, b1, b2,
    o_blk, o_ig, o_fs, o_g1, o_g2, o_b,
    W, XIN, GT, NT, XRT, L, SI, H, HG, UP, PB, SP, G, OUT, BC, BT, BG,
    CR, XRV, YR, FXR, FCR, CSB, YSB, ZSB, FSB,
    in_sem, own_sem, out_sem, b_ssem, b_rsem, g_ssem, g_rsem,
    cs_sem, cr_sem, xs_sem, xr_sem, ys_sem, yr_sem, zs_sem, zr_sem, fs_sem, fr_sem, f2s_sem, f2r_sem,
    bgs_sem, bgr_sem,
):
    dp, w = lax.axis_index("dp"), lax.axis_index("wide")
    x, c = lax.div(dp, 2), lax.rem(dp, 2)
    z, y = lax.div(w, 2), lax.rem(w, 2)
    d_sib = (x * 2 + 1 - c, w)
    d_x = ((1 - x) * 2 + c, w)
    d_y = (dp, z * 2 + 1 - y)
    d_right = (dp, w + 2)
    d_left = (dp, w - 2)
    own_g = c * (1 + x)
    oth_g = c * (2 - x)

    def ring_z(by):
        return lax.rem(z + by, 4)

    barrier = pltpu.get_barrier_semaphore()
    greeted = [d_sib, d_x] + [(dp, lax.rem(w + by, NW)) for by in range(1, NW)]
    for dev in greeted:
        pl.semaphore_signal(barrier, inc=1, device_id=dev, device_id_type=MESH)

    def shard(k, s):
        return pl.ds(al((k * NW + s) * RS), RS)

    def own_copy(k):
        return pltpu.make_async_copy((k1, k2)[k], W.at[shard(k, w)], own_sem.at[k])

    own_copy(0).start()
    own_copy(1).start()
    BT[w] = jnp.zeros((8, LT), F32)
    BT[w, 0:1, 0:CS] = b1[...].astype(F32)
    BT[w, 1:2, 0:CS] = b2[...].astype(F32)
    sources = [xc, xr, gc, gr, nz.at[0], nz.at[1]]

    def in_copy(n):
        return pltpu.make_async_copy(sources[n], XIN.at[n % 2], in_sem.at[n % 2])

    in_copy(0).start()
    in_copy(1).start()
    own_copy(0).wait()
    own_copy(1).wait()
    pl.semaphore_wait(barrier, len(greeted))

    devs = {RIGHT: d_right, LEFT: d_left, YN: d_y, SIB: d_sib, XN: d_x}

    def message(k, s, tap, way):
        part = W.at[pl.ds(al((k * NW + s) * RS + tap * CS), CS)]
        return pltpu.make_async_remote_copy(
            src_ref=part, dst_ref=part, send_sem=g_ssem.at[way], recv_sem=g_rsem.at[k, s, tap],
            device_id=devs[way], device_id_type=MESH,
        )

    def arrive(k, s, tap):
        message(k, s, tap, YN).wait_recv()

    def events(k, m):
        def z_part(n, j):
            tap = own_g * 3 + j

            @pl.when(n == 0)
            def _():
                @pl.when(z < 3)
                def _():
                    message(k, w, tap, RIGHT).start()

                @pl.when(z > 0)
                def _():
                    message(k, w, tap, LEFT).start()

                message(k, w, tap, YN).start()

            def flow(zz, onward, may):
                s = zz * 2 + y
                arrive(k, s, tap)

                @pl.when(may)
                def _():
                    message(k, s, tap, onward).start()

                message(k, s, tap, YN).start()
                message(k, s, tap, SIB).start()

                @pl.when(c == 1)
                def _():
                    message(k, s, tap, XN).start()

            @pl.when((n >= 1) & (z - n >= 0))
            def _():
                flow(z - n, RIGHT, z < 3)

            @pl.when((n >= 1) & (z + n <= 3))
            def _():
                flow(z + n, LEFT, z > 0)

        def y_part(n, j):
            tap = own_g * 3 + j

            def flow(zz):
                s = zz * 2 + 1 - y
                arrive(k, s, tap)
                message(k, s, tap, SIB).start()

                @pl.when(c == 1)
                def _():
                    message(k, s, tap, XN).start()

            @pl.when(z - n >= 0)
            def _():
                flow(z - n)

            @pl.when((n >= 1) & (z + n <= 3))
            def _():
                flow(z + n)

        def x_part(n, j, yy, least):
            tap = oth_g * 3 + j

            def flow(zz):
                s = zz * 2 + yy
                arrive(k, s, tap)
                message(k, s, tap, SIB).start()

            @pl.when((c == 1) & (n >= least) & (z - n >= 0))
            def _():
                flow(z - n)

            @pl.when((c == 1) & (n >= 1) & (z + n <= 3))
            def _():
                flow(z + n)

        for lag, part in (
            (LAG_Y + LAG_X, lambda n, j: x_part(n, j, 1 - y, 0)),
            (LAG_X, lambda n, j: x_part(n, j, y, 1)),
            (LAG_Y, y_part),
            (0, z_part),
        ):
            at = m - lag

            @pl.when((at >= 0) & (at < 12))
            def _(part=part, at=at):
                at = jnp.maximum(at, 0)
                part(lax.div(at, 3), lax.rem(at, 3))

    def ready(k, s):
        @pl.when(s != w)
        def _():
            @pl.when(c == 0)
            def _():
                for tap in range(3, 9):
                    arrive(k, s, tap)

            @pl.when(c == 1)
            def _():
                for tap in range(3):
                    arrive(k, s, tap)

    def bias_message(by):
        return pltpu.make_async_remote_copy(
            src_ref=BT.at[w], dst_ref=BT.at[w], send_sem=b_ssem.at[by], recv_sem=b_rsem.at[w],
            device_id=(dp, lax.rem(w + by, NW)), device_id_type=MESH,
        )

    def bias_arrive(by):
        s = lax.rem(w + by, NW)
        pltpu.make_async_remote_copy(
            src_ref=BT.at[s], dst_ref=BT.at[s], send_sem=b_ssem.at[by], recv_sem=b_rsem.at[s],
            device_id=(dp, s), device_id_type=MESH,
        ).wait_recv()

    events(0, 0)
    for by in range(1, NW):
        bias_message(by).start()

    S0, I0 = 0, C

    for n in range(6):
        in_copy(n).wait()
        if n == 0:
            t = XIN[0].T.astype(F32)
            SI[S0 : S0 + C, :] = t
            L[0] = leak(t).astype(BF16)
        elif n == 1:
            t = XIN[1].T
            XRT[...] = t
            L[1] = leak(t.astype(F32)).astype(BF16)
        elif n < 4:
            GT[n - 2] = XIN[n % 2].T
        else:
            NT[n - 4] = XIN[n % 2].T
        if n + 2 < 6:
            in_copy(n + 2).start()
        events(0, n + 1) if n < 2 else None
    H[...] = jnp.zeros_like(H)
    events(0, 3)
    for by in range(1, NW):
        bias_arrive(by)

    def bias_columns(s, carry):
        for k in range(2):
            row = jnp.broadcast_to(BT[s, k : k + 1, :], (LT, LT))
            BC[k, pl.ds(al(s * CS), CS), :] = row.T[0:CS, :]
        return carry

    lax.fori_loop(0, NW, bias_columns, 0)

    def rows_of(s):
        return pl.ds(al(s * CS), CS)

    def cols(n):
        return slice(n * LT, (n + 1) * LT)

    def patches(load, row):
        for n in range(PX // LT):
            v = load(cols(n))
            for t, (di, dj) in enumerate(TAPS):
                PB[n // 2, row + t * CS : row + (t + 1) * CS, cols(n % 2)] = moved(v, di, dj)

    def held(row):
        return jnp.concatenate([PB[m, row : row + RS, :] for m in range(PX // 256)], axis=1)

    def spread_back(k, s, cot, use):
        for n in range(PX // 256):
            SP[...] = nn(W[shard(k, s)], cot[:, n * 256 : (n + 1) * 256])
            for h in range(2):
                total = None
                for t, (di, dj) in enumerate(TAPS):
                    v = moved(SP[t * CS : (t + 1) * CS, h * LT : (h + 1) * LT], -di, -dj)
                    total = v if total is None else total + v
                use(cols(2 * n + h), total)

    def take_first(s):
        ready(0, s)
        for part in range(2):
            patches(lambda at: L[part, rows_of(s), at], part * RS)
            H[part] += tn(W[shard(0, s)], held(part * RS))

    def take_second(s):
        ready(1, s)

        def chain(at, inner):
            SI[pl.ds(al(I0 + s * CS), CS), at] = inner

        spread_back(1, s, GT.at[0], chain)

        def real(at, inner):
            hid = H[1, rows_of(s), at] + BC[0, rows_of(s), :]
            HG[1, rows_of(s), at] = (inner * slope(hid)).astype(BF16)
            UP[1, rows_of(s), at] = leak(hid).astype(BF16)

        spread_back(1, s, GT.at[1], real)

    def turns(q, take):
        @pl.when((q >= 0) & (q < 12))
        def _():
            n, part = lax.div(jnp.maximum(q, 0), 3), lax.rem(jnp.maximum(q, 0), 3)

            def one(u, carry):
                side, flip = lax.rem(u, 2), lax.div(u, 2)
                zz = z + (2 * side - 1) * n
                yy = y + flip - 2 * y * flip

                @pl.when((zz >= 0) & (zz <= 3) & ((n > 0) | (side == 0)))
                def _():
                    take(zz * 2 + yy)

                return carry

            lax.fori_loop(part, part + 1 + lax.div(part, 2), one, 0)

    def slot(r, carry):
        events(0, r)
        events(1, r - 12)
        turns(r - LAG_T, take_first)
        turns(r - 12 - LAG_T, take_second)
        return carry

    lax.fori_loop(4, 24 + LAG_T, slot, 0)

    def tile(n):
        return slice(n * 256, (n + 1) * 256)

    def half_tiles(n):
        return [(h, cols(2 * n + h), cols(h)) for h in range(2)]

    def shard_rows(s, base=0):
        return slice(base + s * CS, base + (s + 1) * CS)

    def step_state(k, n):
        for s in range(NW):
            rows = shard_rows(s)
            for h, at, to in half_tiles(n):
                state = SI[shard_rows(s, S0), at]
                pull = GT[0, rows, at].astype(F32) + slope(state) * H[0, rows, at]
                state = state - pull + 0.01 * NT[k, rows, at].astype(F32)
                SI[shard_rows(s, S0), at] = state
                low = leak(state).astype(BF16)
                L[0, rows, at] = low
                for t, (di, dj) in enumerate(TAPS):
                    PB[n, s * RS + t * CS : s * RS + (t + 1) * CS, to] = moved(low, di, dj)

    def hidden_grad(n, sign, last, patch):
        for s in range(NW):
            rows = shard_rows(s)
            for h, at, to in half_tiles(n):
                hid = H[0, rows, at] + BC[0, rows, :]
                grad = SI[shard_rows(s, I0), at] * slope(hid)
                grad = (grad if sign is None else grad * sign).astype(BF16)
                HG[0, rows, at] = grad
                if last:
                    UP[0, rows, at] = leak(hid).astype(BF16)
                if patch:
                    for t, (di, dj) in enumerate(TAPS):
                        PB[n, t * C + s * CS : t * C + (s + 1) * CS, to] = moved(grad, -di, -dj)

    def product_first(n):
        total = None
        for at in range(0, NW * RS, 2 * C):
            rows = slice(at, min(at + 2 * C, NW * RS))
            part = tn(W[rows, :], PB[n, rows, :])
            total = part if total is None else total + part
        H[0, :, tile(n)] = total

    def product_back(n):
        total = None
        for t in range(0, 9, 2):
            left = jnp.concatenate(
                [
                    jnp.concatenate([W[s * RS + u * CS : s * RS + (u + 1) * CS, :] for s in range(NW)], axis=0)
                    for u in range(t, min(t + 2, 9))
                ],
                axis=1,
            )
            part = nn(left, PB[n, t * C : min(t + 2, 9) * C, :])
            total = part if total is None else total + part
        H[0, :, tile(n)] = total

    hidden_grad(0, None, False, True)

    def langevin(k, carry):
        hidden_grad(1, None, False, True)
        product_back(0)
        hidden_grad(2, None, False, True)
        product_back(1)
        step_state(k, 0)
        product_back(2)
        step_state(k, 1)
        product_first(0)
        step_state(k, 2)
        product_first(1)
        hidden_grad(0, (1 - 2 * k).astype(F32), True, True)
        product_first(2)
        return carry

    lax.fori_loop(0, 2, langevin, 0)
    hidden_grad(1, -1.0, True, False)
    hidden_grad(2, -1.0, True, False)
    for n in range(PX // LT):
        GT[0, :, cols(n)] = -GT[0, :, cols(n)]
    OUT[...] = SI[S0 : S0 + C, :].T

    def out_copy(ref, rows=PX):
        return pltpu.make_async_copy(OUT.at[0:rows], ref, out_sem)

    out_copy(o_fs).start()

    ones = jnp.ones((8, PX), BF16)
    BG[0, 0:8, :] = nt(ones, HG[0]) + nt(ones, HG[1])
    BG[0, 8:16, :] = nt(ones, GT[0]) + nt(ones, GT[1])

    def bg_send(src, dst, sem, dev):
        return pltpu.make_async_remote_copy(
            src_ref=BG.at[src], dst_ref=BG.at[dst], send_sem=bgs_sem.at[sem], recv_sem=bgr_sem.at[sem],
            device_id=dev, device_id_type=MESH,
        )

    def bg_step(i):
        @pl.when(i == 1)
        def _():
            bg_send(0, 3, 0, d_sib).start()

        @pl.when(i == 2)
        def _():
            bg_send(0, 3, 0, d_sib).wait()
            BG[1] = BG[0] + BG[3]
            bg_send(1, 4, 1, d_x).start()

        @pl.when(i == 4)
        def _():
            bg_send(1, 4, 1, d_x).wait()
            BG[2] = BG[1] + BG[4]
            bg_send(2, 5, 2, d_y).start()

        @pl.when(i == 6)
        def _():
            bg_send(2, 5, 2, d_y).wait()
            BG[6 + z] = BG[2] + BG[5]
            for by in range(1, 4):
                bg_send(6 + z, 6 + z, 2 + by, (dp, ring_z(by) * 2 + y)).start()

        @pl.when(i == 9)
        def _():
            for by in range(1, 4):
                bg_send(6 + z, 6 + z, 2 + by, (dp, ring_z(by) * 2 + y)).wait()
            BG[0] = BG[6] + BG[7] + BG[8] + BG[9]
            pltpu.make_async_copy(BG.at[0], o_b, own_sem.at[3]).start()

    def places(pair):
        return 2 - pair + 3 * lax.div(pair, 2) - 2 * lax.div(pair, 3)

    def shard_of(a):
        p = lax.rem(a, 8)
        zz = ring_z(places(lax.div(p, 2)))
        yy = lax.rem(y + 1 + lax.rem(p, 2), 2)
        return zz, yy

    def both_held():
        return jnp.concatenate([held(0), held(RS)], axis=1)

    def first_block(s, buf):
        for part in range(2):
            patches(lambda at: L[part, rows_of(s), at], part * RS)
        G[buf] = nt(both_held(), jnp.concatenate([HG[0], HG[1]], axis=1))

        def keep(at, total):
            H[0, rows_of(s), at] = total

        spread_back(0, s, HG.at[1], keep)

    def second_block(s, buf, start):
        for part in range(2):
            patches(lambda at: UP[part, rows_of(s), at], part * RS)
        G[buf] = nt(both_held(), jnp.concatenate([GT[0], GT[1]], axis=1))
        add = tn(W[shard(1, s)], held(RS))

        @pl.when(start)
        def _():
            H[1] = add

        @pl.when(jnp.logical_not(start))
        def _():
            H[1] += add

    def remote(src, dst, ss, rs, dev):
        return pltpu.make_async_remote_copy(
            src_ref=src, dst_ref=dst, send_sem=ss, recv_sem=rs, device_id=dev, device_id_type=MESH
        )

    def core_send(a, core):
        q, h = lax.rem(a, 4), lax.rem(a, 2)
        rows = 2 * GR if core == 0 else GR
        return remote(CSB.at[h, 0:rows], CR.at[q, 0:rows], cs_sem.at[h], cr_sem.at[q], d_sib)

    def tap(j):
        return slice(j * CS, (j + 1) * CS)

    def x_out(h, j):
        return lax.div(h, 2), pl.ds(al(lax.rem(h, 2) * GR + j * CS), CS), slice(0, C)

    def x_send(a, j):
        q, h = lax.rem(a, XSLOTS), lax.rem(a, 4)
        return remote(NT.at[x_out(h, j)], XRV.at[q, tap(j)], xs_sem.at[h, j], xr_sem.at[q, j], d_x)

    def y_send(a, zz, j):
        q = lax.rem(lax.div(a, 2), 2)
        return remote(YSB.at[q, tap(j)], YR.at[zz, tap(j)], ys_sem.at[q, j], yr_sem.at[zz, j], d_y)

    def z_send(a, by, j):
        q = lax.rem(lax.div(a, 2), 2)
        land = XIN.at[lax.div(a, 8), pl.ds(al((by - 1) * GR + j * CS), CS), :]
        return remote(
            ZSB.at[q, tap(j)], land, zs_sem.at[q, j], zr_sem.at[lax.div(a, 8), by - 1, j], (dp, ring_z(by) * 2 + y)
        )

    def f_send(turn_, j):
        return remote(FSB.at[tap(j)], FXR.at[turn_, tap(j)], fs_sem.at[turn_, j], fr_sem.at[turn_, j], d_x)

    def f2_send(turn_, src, row, j, n):
        to = FCR.at[pl.ds(al(row + j * CS), CS)]
        return remote(src.at[tap(j)], to, f2s_sem.at[turn_, n, j], f2r_sem.at[turn_, n, j], d_sib)

    def acc(a, j):
        half, odd = lax.div(a, 2), lax.rem(a, 2)
        slot_ = lax.rem(half, 2) * (1 - odd) + (2 + lax.rem(half, 3)) * odd
        return pl.ds(al(slot_ * GR + j * CS), CS)

    def reduce_step(i, carry):
        @pl.when(i < 16)
        def _():
            zz, yy = shard_of(i)
            s = zz * 2 + yy
            buf, h = lax.rem(i, 2), lax.rem(i, 2)

            @pl.when(i < 8)
            def _():
                second_block(s, buf, i == 0)

            @pl.when(i >= 8)
            def _():
                first_block(s, buf)

            for core in range(2):

                @pl.when(c == core)
                def _(core=core):
                    @pl.when(i >= 2)
                    def _():
                        core_send(i - 2, core).wait_send()

                    if core == 0:
                        CSB[h] = G[buf, GR : 3 * GR, :].astype(BF16)
                    else:
                        CSB[h, 0:GR] = G[buf, 0:GR, :].astype(BF16)
                    core_send(i, core).start()

        @pl.when((i >= 1) & (i < 17))
        def _():
            a = i - 1
            q, h, buf = lax.rem(a, 4), lax.rem(a, 4), lax.rem(a, 2)

            @pl.when(c == 0)
            def _():
                core_send(a, 1).wait_recv()
                for j in range(3):
                    SI[acc(a, j), 0:C] = G[buf, tap(j), :] + CR[q, tap(j), :].astype(F32)

            @pl.when(c == 1)
            def _():
                core_send(a, 0).wait_recv()

                def theirs(g, j):
                    return (
                        G[buf, pl.ds(al(g * GR + j * CS), CS), :]
                        + CR[q, pl.ds(al(jnp.maximum(g - 1, 0) * GR + j * CS), CS), :].astype(F32)
                    )

                for j in range(3):

                    @pl.when(a >= 4)
                    def _(j=j):
                        x_send(a - 4, j).wait_send()

                    NT[x_out(h, j)] = theirs(oth_g, j).astype(BF16)
                    x_send(a, j).start()
                for j in range(3):
                    SI[acc(a, j), 0:C] = theirs(own_g, j)

        @pl.when((i >= LAG_C) & (i < 16 + LAG_C))
        def _():
            a = i - LAG_C
            zz, yy = shard_of(a)
            q = lax.rem(lax.div(a, 2), 2)
            for j in range(3):

                @pl.when(c == 1)
                def _(j=j):
                    x_send(a, j).wait_recv()
                    SI[acc(a, j), 0:C] += XRV[lax.rem(a, XSLOTS), tap(j)].astype(F32)

                @pl.when(lax.rem(a, 2) == 0)
                def _(j=j):
                    @pl.when(a >= 4)
                    def _():
                        y_send(a - 4, 0, j).wait_send()

                    YSB[q, tap(j)] = SI[acc(a, j), 0:C].astype(BF16)
                    y_send(a, zz, j).start()

        @pl.when((i >= LAG_D + 1) & (i < 16 + LAG_D) & (lax.rem(i + LAG_D, 2) == 1))
        def _():
            a = i - LAG_D
            zz, yy = shard_of(a)
            pair = lax.div(lax.rem(a, 8), 2)
            q, turn_ = lax.rem(lax.div(a, 2), 2), lax.div(a, 8)
            for j in range(3):
                y_send(a, zz, j).wait_recv()
                total = SI[acc(a, j), 0:C] + YR[zz, tap(j)].astype(F32)

                @pl.when(pair < 3)
                def _(j=j, total=total):
                    @pl.when(a >= 5)
                    def _():
                        z_send(a, 1, j).wait_send()

                    ZSB[q, tap(j)] = total.astype(BF16)
                    for by in range(1, 4):

                        @pl.when(places(pair) == by)
                        def _(by=by):
                            z_send(a, by, j).start()

                @pl.when(pair == 3)
                def _(j=j, total=total):
                    whole = total
                    for by in range(1, 4):
                        z_send(a, by, j).wait_recv()
                        at = slice((by - 1) * GR + j * CS, (by - 1) * GR + (j + 1) * CS)
                        whole = whole + XIN[turn_, at, :].astype(F32)
                    FSB[tap(j)] = whole.astype(BF16)
                    f_send(turn_, j).start()

        for turn_, ref in ((0, o_g2), (1, o_g1)):
            base = 8 * turn_

            @pl.when(i == base + F2)
            def _(turn_=turn_):
                for j in range(3):
                    f_send(turn_, j).wait()

                    @pl.when(c == 0)
                    def _(j=j):
                        both = FSB[tap(j)].astype(F32) + FXR[turn_, tap(j)].astype(F32)
                        FSB[tap(j)] = both.astype(BF16)
                        f2_send(turn_, FSB, 0, j, 0).start()

                    @pl.when(c == 1)
                    def _(j=j):
                        f2_send(turn_, FSB, (own_g - 1) * GR, j, own_g - 1).start()
                        f2_send(turn_, FXR.at[turn_], (oth_g - 1) * GR, j, oth_g - 1).start()

            @pl.when(i == base + F3)
            def _(turn_=turn_, ref=ref):
                out_copy(o_fs).wait()

                @pl.when(c == 0)
                def _():
                    for j in range(3):
                        OUT[tap(j), :] = FSB[tap(j)].astype(F32)
                    for n in range(2):
                        for j in range(3):
                            f2_send(turn_, FSB, n * GR, j, n).wait_recv()
                            at = slice(n * GR + j * CS, n * GR + (j + 1) * CS)
                            OUT[GR + n * GR + j * CS : GR + n * GR + (j + 1) * CS, :] = FCR[at].astype(F32)
                    for j in range(3):
                        f2_send(turn_, FSB, 0, j, 0).wait_send()

                @pl.when(c == 1)
                def _():
                    OUT[pl.ds(al(jnp.maximum(own_g, 1) * GR), GR), :] = FSB[...].astype(F32)
                    OUT[pl.ds(al(jnp.maximum(oth_g, 1) * GR), GR), :] = FXR[turn_].astype(F32)
                    for j in range(3):
                        f2_send(turn_, FSB, 0, j, 0).wait_recv()
                        OUT[tap(j), :] = FCR[tap(j)].astype(F32)
                    for j in range(3):
                        f2_send(turn_, FSB, 0, j, own_g - 1).wait_send()
                        f2_send(turn_, FXR.at[turn_], 0, j, oth_g - 1).wait_send()

                out_copy(ref, RS).start()

        @pl.when(i == 8)
        def _():
            out_copy(o_fs).wait()
            for n in range(PX // LT):
                whole = XRT[:, cols(n)].astype(F32) + H[1, :, cols(n)] + BC[1]
                OUT[n * LT : (n + 1) * LT, :] = whole.T
            out_copy(o_blk).start()

        @pl.when(i == 16)
        def _():
            out_copy(o_g2, RS).wait()
            for n in range(PX // LT):
                whole = GT[1, :, cols(n)].astype(F32) + slope(XRT[:, cols(n)].astype(F32)) * H[0, :, cols(n)]
                OUT[n * LT : (n + 1) * LT, :] = whole.T
            out_copy(o_ig).start()

        bg_step(i)
        return carry

    lax.fori_loop(0, 8 + F3 + 1, reduce_step, 0)

    out_copy(o_g1, RS).wait()
    pltpu.make_async_copy(BG.at[0], o_b, own_sem.at[3]).wait()
    for by in range(1, NW):
        bias_message(by).wait_send()

    def drain(way, planes, rows):
        part = W.at[0 : planes * rows]
        remote(part, part, g_ssem.at[way], g_rsem.at[0, 0, 0], d_sib).wait_send()

    for zz in range(4):

        @pl.when(z == zz)
        def _(zz=zz):
            if zz < 3:
                drain(RIGHT, 2 * (zz + 1), GR)
            if zz > 0:
                drain(LEFT, 2 * (4 - zz), GR)

    drain(YN, 8, GR)

    @pl.when(c == 0)
    def _():
        drain(SIB, 14, GR)
        for a in range(14, 16):
            core_send(a, 0).wait_send()

    @pl.when(c == 1)
    def _():
        drain(SIB, 14, 2 * GR)
        drain(XN, 14, GR)
        for a in range(14, 16):
            core_send(a, 1).wait_send()
        for a in range(12, 16):
            for j in range(3):
                x_send(a, j).wait_send()

    for j in range(3):
        for a in (12, 14):
            y_send(a, 0, j).wait_send()
        for a in (11, 13):
            z_send(a, 1, j).wait_send()


PIECES = 3


def hand_over(blk, ig, fs, g1, g2, bsum, o_blk, o_ig, o_fs, o_g1, o_g2, o_b1, o_b2, wide, tall, sem):
    loads, stores = [], []
    for n, (src, dst) in enumerate(((blk, o_blk), (ig, o_ig), (fs, o_fs), (g1, o_g1), (g2, o_g2))):
        rows = src.shape[0] // PIECES
        for p in range(PIECES):
            at = pl.ds(p * rows, rows)
            held = wide.at[n, at] if n < 3 else tall.at[n - 3, at]
            loads.append(pltpu.make_async_copy(src.at[at], held, sem.at[0, n, p]))
            stores.append(pltpu.make_async_copy(held, dst.at[at], sem.at[1, n, p]))
            loads[-1].start()
    w = lax.axis_index("wide")
    for s in range(NW):

        @pl.when(w == s)
        def _(s=s):
            o_b1[...] = bsum[0:1, s * CS : (s + 1) * CS]
            o_b2[...] = bsum[8:9, s * CS : (s + 1) * CS]

    for load, store in zip(loads, stores):
        load.wait()
        store.start()
    for store in stores:
        store.wait()


def kernel_local(real_images, replay_chains, langevin_noise, real_cot, chain_cot, kernel_one, bias_one, kernel_two, bias_two):
    def flat(values):
        return values.reshape(values.shape[:-4] + (PX, C))

    anywhere = pl.BlockSpec(memory_space=pl.ANY)
    dma = pltpu.SemaphoreType.DMA
    out_shape = [jax.ShapeDtypeStruct((PX, C), F32)] * 3 + [jax.ShapeDtypeStruct((RS, C), F32)] * 2
    out_shape += [jax.ShapeDtypeStruct((16, C), F32)]
    scratch = [
        pltpu.VMEM((2 * NW * RS, C), BF16),
        pltpu.VMEM((2, PX, C), BF16),
        pltpu.VMEM((2, C, PX), BF16),
        pltpu.VMEM((2, C, PX), BF16),
        pltpu.VMEM((C, PX), BF16),
        pltpu.VMEM((2, C, PX), BF16),
        pltpu.VMEM((2 * C, PX), F32),
        pltpu.VMEM((2, C, PX), F32),
        pltpu.VMEM((2, C, PX), BF16),
        pltpu.VMEM((2, C, PX), BF16),
        pltpu.VMEM((PX // 256, NW * RS, 256), BF16),
        pltpu.VMEM((RS, 256), F32),
        pltpu.VMEM((2, RS, C), F32),
        pltpu.VMEM((PX, C), F32),
        pltpu.VMEM((2, C, LT), F32),
        pltpu.VMEM((NW, 8, LT), F32),
        pltpu.VMEM((10, 16, C), F32),
        pltpu.VMEM((4, 2 * GR, C), BF16),
        pltpu.VMEM((XSLOTS, GR, C), BF16),
        pltpu.VMEM((4, GR, C), BF16),
        pltpu.VMEM((2, GR, C), BF16),
        pltpu.VMEM((2 * GR, C), BF16),
        pltpu.VMEM((2, 2 * GR, C), BF16),
        pltpu.VMEM((2, GR, C), BF16),
        pltpu.VMEM((2, GR, C), BF16),
        pltpu.VMEM((GR, C), BF16),
        dma((2,)), dma((4,)), dma, dma((NW,)), dma((NW,)), dma((5,)), dma((2, NW, 9)),
        dma((2,)), dma((4,)), dma((4, 3)), dma((XSLOTS, 3)), dma((2, 3)), dma((4, 3)), dma((2, 3)), dma((2, 3, 3)),
        dma((2, 3)), dma((2, 3)), dma((2, 2, 3)), dma((2, 2, 3)), dma((6,)), dma((6,)),
    ]
    made = pl.pallas_call(
        body,
        out_shape=out_shape,
        in_specs=[anywhere] * 7 + [pl.BlockSpec(memory_space=pltpu.VMEM)] * 2,
        out_specs=[anywhere] * 6,
        scratch_shapes=scratch,
        compiler_params=pltpu.CompilerParams(
            collective_id=0, has_side_effects=True, vmem_limit_bytes=65400 * 2**10
        ),
    )(
        flat(real_images), flat(replay_chains), flat(langevin_noise), flat(real_cot), flat(chain_cot),
        kernel_one.reshape(RS, C), kernel_two.reshape(RS, C), bias_one.reshape(1, CS), bias_two.reshape(1, CS),
    )
    blk, ig, fs, g1, g2, first_bias, second_bias = pl.pallas_call(
        hand_over,
        out_shape=out_shape[:5] + [jax.ShapeDtypeStruct((1, CS), F32)] * 2,
        in_specs=[anywhere] * 5 + [pl.BlockSpec(memory_space=pltpu.VMEM)],
        out_specs=[anywhere] * 5 + [pl.BlockSpec(memory_space=pltpu.VMEM)] * 2,
        scratch_shapes=[pltpu.VMEM((3, PX, C), F32), pltpu.VMEM((2, RS, C), F32), dma((2, 5, PIECES))],
    )(*made)
    shape = real_images.shape
    return (
        blk.reshape(shape), ig.reshape(shape), fs.reshape(shape),
        g1.reshape(kernel_one.shape), first_bias.reshape(CS),
        g2.reshape(kernel_two.shape), second_bias.reshape(CS),
    )


def solution(mesh):
    def local(real_images, *rest):
        kernel_one = rest[4]
        fits = (
            mesh.shape["dp"] == 4
            and mesh.shape["wide"] == NW
            and real_images.shape == (12, 8, 8, C)
            and kernel_one.shape == (3, 3, CS, C)
            and rest[1].shape[0] == 2
        )
        return (kernel_local if fits else plain_local)(real_images, *rest)

    return jax.shard_map(
        local,
        mesh=mesh,
        in_specs=(
            P(("dp", "wide"), None, None, None),
            P(("dp", "wide"), None, None, None),
            P(None, ("dp", "wide"), None, None, None),
            P(("dp", "wide"), None, None, None),
            P(("dp", "wide"), None, None, None),
            P(None, None, "wide", None),
            P("wide"),
            P(None, None, "wide", None),
            P("wide"),
        ),
        out_specs=(
            P(("dp", "wide"), None, None, None),
            P(("dp", "wide"), None, None, None),
            P(("dp", "wide"), None, None, None),
            P(None, None, "wide", None),
            P("wide"),
            P(None, None, "wide", None),
            P("wide"),
        ),
        check_vma=False,
    )
```

```python
import functools

import jax
import jax.numpy as jnp
from jax import lax
from jax.experimental import pallas as pl
from jax.experimental.pallas import tpu as pltpu
from jax.sharding import PartitionSpec as P

F32 = jnp.float32
BF16 = jnp.bfloat16
MESH = pl.DeviceIdType.MESH


def leaky_relu(values):
    return jnp.where(values > 0, values, 0.2 * values)


def leak_slope(values):
    return jnp.where(values > 0, 1.0, 0.2).astype(F32)


def tap_patches(activation):
    batch_size, height, map_width, channels = activation.shape
    padded = jnp.pad(activation, ((0, 0), (1, 1), (1, 1), (0, 0)))
    tap_list = [
        padded[:, row_off : row_off + height, col_off : col_off + map_width, :]
        for row_off in range(3)
        for col_off in range(3)
    ]
    return jnp.stack(tap_list, axis=3).reshape(batch_size * height * map_width, 9 * channels)


def conv_apply(activation, kernel_mat, bias_row):
    result = jnp.dot(tap_patches(activation), kernel_mat, preferred_element_type=F32)
    return result.reshape(activation.shape[:3] + (kernel_mat.shape[1],)) + bias_row.astype(F32)


def conv_back(gradient, kernel_mat):
    batch_size, height, map_width, channels = gradient.shape
    in_channels = kernel_mat.shape[0] // 9
    spread = lax.dot_general(
        gradient.reshape(-1, channels), kernel_mat, (((1,), (1,)), ((), ())), preferred_element_type=F32
    )
    spread = spread.reshape(batch_size, height, map_width, 9, in_channels)
    summed = jnp.zeros((batch_size, height + 2, map_width + 2, in_channels), F32)
    for row_off in range(3):
        for col_off in range(3):
            summed = summed + jnp.pad(
                spread[:, :, :, 3 * row_off + col_off, :],
                ((0, 0), (row_off, 2 - row_off), (col_off, 2 - col_off), (0, 0)),
            )
    return summed[:, 1 : height + 1, 1 : map_width + 1, :]


def kernel_partial(activation, gradient):
    channels = gradient.shape[3]
    return lax.dot_general(
        tap_patches(activation),
        gradient.reshape(-1, channels),
        (((0,), (0,)), ((), ())),
        preferred_element_type=F32,
    )


def plain_local(real_images, replay_chains, langevin_noise, real_cot, chain_cot, kernel_one, bias_one, kernel_two, bias_two):
    def whole(kernel):
        gathered = lax.all_gather(kernel, "wide", axis=2, tiled=True)
        return gathered.reshape(9 * gathered.shape[2], gathered.shape[3])

    first, second = whole(kernel_one), whole(kernel_two)
    first_bias = lax.all_gather(bias_one, "wide", axis=0, tiled=True)
    second_bias = lax.all_gather(bias_two, "wide", axis=0, tiled=True)

    def hidden_of(values):
        lower = leaky_relu(values).astype(BF16)
        return lower, conv_apply(lower, first, first_bias)

    def x_grad(values, cot, hidden_grad):
        return cot.astype(F32) + leak_slope(values) * conv_back(hidden_grad, first)

    chain_inner = conv_back(chain_cot, second)
    state = replay_chains.astype(F32)
    for step_index in range(langevin_noise.shape[0]):
        _, hidden = hidden_of(state)
        hidden_grad = (chain_inner * leak_slope(hidden)).astype(BF16)
        state = state - x_grad(state, chain_cot, hidden_grad) + 0.01 * langevin_noise[step_index].astype(F32)
    real = real_images.astype(F32)
    real_lower, real_hidden = hidden_of(real)
    real_upper = leaky_relu(real_hidden).astype(BF16)
    block_output = real + conv_apply(real_upper, second, second_bias)
    sample_lower, sample_hidden = hidden_of(state)
    sample_upper = leaky_relu(sample_hidden).astype(BF16)
    real_hgrad = (conv_back(real_cot, second) * leak_slope(real_hidden)).astype(BF16)
    input_grad = x_grad(real, real_cot, real_hgrad)
    sample_hgrad = -((chain_inner * leak_slope(sample_hidden)).astype(BF16))

    def bias_sum(values):
        return jnp.sum(values.astype(F32), axis=(0, 1, 2))

    totals = (
        kernel_partial(real_lower, real_hgrad) + kernel_partial(sample_lower, sample_hgrad),
        bias_sum(real_hgrad) + bias_sum(sample_hgrad),
        kernel_partial(real_upper, real_cot) + kernel_partial(sample_upper, -chain_cot),
        bias_sum(real_cot) - bias_sum(chain_cot),
    )
    channels = kernel_one.shape[3]
    kernel_shape = (3, 3, channels, channels)
    shares = (
        lax.psum_scatter(totals[0].reshape(kernel_shape), "wide", scatter_dimension=2, tiled=True),
        lax.psum_scatter(totals[1], "wide", scatter_dimension=0, tiled=True),
        lax.psum_scatter(totals[2].reshape(kernel_shape), "wide", scatter_dimension=2, tiled=True),
        lax.psum_scatter(totals[3], "wide", scatter_dimension=0, tiled=True),
    )
    summed = lax.psum(shares, "dp")
    return (block_output, input_grad, state, summed[0], summed[1], summed[2], summed[3])


NW = 8
C = 640
CS = C // NW
PX = 768
RS = 9 * CS
GR = 3 * CS
LT = 128
TAPS = [(p - 1, q - 1) for p in range(3) for q in range(3)]

LAG_C, LAG_D = 3, 5
XSLOTS = 2 * LAG_C - 2
F2 = 8 + LAG_D
F3 = F2 + 1
FILL, TAIL = 1, 16

RIGHT, LEFT, YN, SIB, XN = range(5)
LAG_Y, LAG_X = 4, 4
LAG_T = max(LAG_X, LAG_Y + LAG_X - 1) + 3


def tn(a, b):
    return lax.dot_general(a, b, (((0,), (0,)), ((), ())), preferred_element_type=F32)


def nt(a, b):
    return lax.dot_general(a, b, (((1,), (1,)), ((), ())), preferred_element_type=F32)


def nn(a, b):
    return jnp.dot(a, b, preferred_element_type=F32)


def leak(v):
    return jnp.where(v > 0, v, 0.2 * v)


def slope(v):
    return jnp.where(v > 0, 1.0, 0.2).astype(F32)


def inside(di, dj):
    lane = lax.broadcasted_iota(jnp.int32, (1, LT), 1)
    row, col = (lane // 8) % 8 + di, lane % 8 + dj
    return (row >= 0) & (row < 8) & (col >= 0) & (col < 8)


def turn(v, by):
    by %= LT
    return v if by == 0 else pltpu.roll(v, by, 1)


def moved(v, di, dj):
    if di == 0 and dj == 0:
        return v
    return jnp.where(inside(di, dj), turn(v, -(8 * di + dj)), jnp.zeros_like(v))


def al(row, by=16):
    return pl.multiple_of(row, by)


def body(
    xr, xc, nz, gr, gc, k1, k2, b1, b2,
    o_blk, o_ig, o_fs, o_g1, o_g2, o_b,
    W, XIN, GT, NT, XRT, L, SI, H, HG, UP, PB, SP, G, OUT, BC, BT, BG,
    CR, XRV, YR, FXR, FCR, CSB, YSB, ZSB, FSB,
    in_sem, own_sem, out_sem, b_ssem, b_rsem, g_ssem, g_rsem,
    cs_sem, cr_sem, xs_sem, xr_sem, ys_sem, yr_sem, zs_sem, zr_sem, fs_sem, fr_sem, f2s_sem, f2r_sem,
    bgs_sem, bgr_sem,
):
    dp, w = lax.axis_index("dp"), lax.axis_index("wide")
    x, c = lax.div(dp, 2), lax.rem(dp, 2)
    z, y = lax.div(w, 2), lax.rem(w, 2)
    d_sib = (x * 2 + 1 - c, w)
    d_x = ((1 - x) * 2 + c, w)
    d_y = (dp, z * 2 + 1 - y)
    z_hi, z_lo = lax.div(z, 2), lax.rem(z, 2)
    d_z1 = (dp, (2 * z_hi + 1 - z_lo) * 2 + y)
    d_z2 = (dp, (2 * (1 - z_hi) + z_lo) * 2 + y)
    d_right = (dp, w + 2)
    d_left = (dp, w - 2)
    own_g = c * (1 + x)
    oth_g = c * (2 - x)

    def ring_z(by):
        return lax.rem(z + by, 4)

    barrier = pltpu.get_barrier_semaphore()
    greeted = [d_sib, d_x] + [(dp, lax.rem(w + by, NW)) for by in range(1, NW)]
    for dev in greeted:
        pl.semaphore_signal(barrier, inc=1, device_id=dev, device_id_type=MESH)

    def shard(k, s):
        return pl.ds(al((k * NW + s) * RS), RS)

    def own_copy(k):
        return pltpu.make_async_copy((k1, k2)[k], W.at[shard(k, w)], own_sem.at[k])

    own_copy(0).start()
    own_copy(1).start()
    BT[w] = jnp.zeros((8, LT), F32)
    BT[w, 0:1, 0:CS] = b1[...].astype(F32)
    BT[w, 1:2, 0:CS] = b2[...].astype(F32)
    sources = [xc, xr, gc, gr, nz.at[0], nz.at[1]]

    def in_copy(n):
        return pltpu.make_async_copy(sources[n], XIN.at[n % 2], in_sem.at[n % 2])

    in_copy(0).start()
    in_copy(1).start()
    own_copy(0).wait()
    own_copy(1).wait()
    pl.semaphore_wait(barrier, len(greeted))

    devs = {RIGHT: d_right, LEFT: d_left, YN: d_y, SIB: d_sib, XN: d_x}

    def message(k, s, tap, way):
        part = W.at[pl.ds(al((k * NW + s) * RS + tap * CS), CS)]
        return pltpu.make_async_remote_copy(
            src_ref=part, dst_ref=part, send_sem=g_ssem.at[way], recv_sem=g_rsem.at[k, s, tap],
            device_id=devs[way], device_id_type=MESH,
        )

    def arrive(k, s, tap):
        message(k, s, tap, YN).wait_recv()

    def events(k, m):
        def z_part(n, j):
            tap = own_g * 3 + j

            @pl.when(n == 0)
            def _():
                @pl.when(z < 3)
                def _():
                    message(k, w, tap, RIGHT).start()

                @pl.when(z > 0)
                def _():
                    message(k, w, tap, LEFT).start()

                message(k, w, tap, YN).start()

            def flow(zz, onward, may):
                s = zz * 2 + y
                arrive(k, s, tap)

                @pl.when(may)
                def _():
                    message(k, s, tap, onward).start()

                message(k, s, tap, YN).start()
                message(k, s, tap, SIB).start()

                @pl.when(c == 1)
                def _():
                    message(k, s, tap, XN).start()

            @pl.when((n >= 1) & (z - n >= 0))
            def _():
                flow(z - n, RIGHT, z < 3)

            @pl.when((n >= 1) & (z + n <= 3))
            def _():
                flow(z + n, LEFT, z > 0)

        def y_part(n, j):
            tap = own_g * 3 + j

            def flow(zz):
                s = zz * 2 + 1 - y
                arrive(k, s, tap)
                message(k, s, tap, SIB).start()

                @pl.when(c == 1)
                def _():
                    message(k, s, tap, XN).start()

            @pl.when(z - n >= 0)
            def _():
                flow(z - n)

            @pl.when((n >= 1) & (z + n <= 3))
            def _():
                flow(z + n)

        def x_part(n, j, yy, least):
            tap = oth_g * 3 + j

            def flow(zz):
                s = zz * 2 + yy
                arrive(k, s, tap)
                message(k, s, tap, SIB).start()

            @pl.when((c == 1) & (n >= least) & (z - n >= 0))
            def _():
                flow(z - n)

            @pl.when((c == 1) & (n >= 1) & (z + n <= 3))
            def _():
                flow(z + n)

        for lag, part in (
            (LAG_Y + LAG_X, lambda n, j: x_part(n, j, 1 - y, 0)),
            (LAG_X, lambda n, j: x_part(n, j, y, 1)),
            (LAG_Y, y_part),
            (0, z_part),
        ):
            at = m - lag

            @pl.when((at >= 0) & (at < 12))
            def _(part=part, at=at):
                at = jnp.maximum(at, 0)
                part(lax.div(at, 3), lax.rem(at, 3))

    def ready(k, s):
        @pl.when(s != w)
        def _():
            @pl.when(c == 0)
            def _():
                for tap in range(3, 9):
                    arrive(k, s, tap)

            @pl.when(c == 1)
            def _():
                for tap in range(3):
                    arrive(k, s, tap)

    def bias_message(by):
        return pltpu.make_async_remote_copy(
            src_ref=BT.at[w], dst_ref=BT.at[w], send_sem=b_ssem.at[by], recv_sem=b_rsem.at[w],
            device_id=(dp, lax.rem(w + by, NW)), device_id_type=MESH,
        )

    def bias_arrive(by):
        s = lax.rem(w + by, NW)
        pltpu.make_async_remote_copy(
            src_ref=BT.at[s], dst_ref=BT.at[s], send_sem=b_ssem.at[by], recv_sem=b_rsem.at[s],
            device_id=(dp, s), device_id_type=MESH,
        ).wait_recv()

    events(0, 0)
    for by in range(1, NW):
        bias_message(by).start()

    S0, I0 = 0, C

    for n in range(6):
        in_copy(n).wait()
        if n == 0:
            t = XIN[0].T.astype(F32)
            SI[S0 : S0 + C, :] = t
            L[0] = leak(t).astype(BF16)
        elif n == 1:
            t = XIN[1].T
            XRT[...] = t
            L[1] = leak(t.astype(F32)).astype(BF16)
        elif n < 4:
            GT[n - 2] = XIN[n % 2].T
        else:
            NT[n - 4] = XIN[n % 2].T
        if n + 2 < 6:
            in_copy(n + 2).start()
        events(0, n + 1) if n < 2 else None
    H[...] = jnp.zeros_like(H)
    events(0, 3)
    for by in range(1, NW):
        bias_arrive(by)

    def bias_columns(s, carry):
        for k in range(2):
            row = jnp.broadcast_to(BT[s, k : k + 1, :], (LT, LT))
            BC[k, pl.ds(al(s * CS), CS), :] = row.T[0:CS, :]
        return carry

    lax.fori_loop(0, NW, bias_columns, 0)

    def rows_of(s):
        return pl.ds(al(s * CS), CS)

    def cols(n):
        return slice(n * LT, (n + 1) * LT)

    def patches(load, row):
        for n in range(PX // LT):
            v = load(cols(n))
            for t, (di, dj) in enumerate(TAPS):
                PB[n // 2, row + t * CS : row + (t + 1) * CS, cols(n % 2)] = moved(v, di, dj)

    def held(row):
        return jnp.concatenate([PB[m, row : row + RS, :] for m in range(PX // 256)], axis=1)

    def spread_back(k, s, cot, use):
        for n in range(PX // 256):
            SP[...] = nn(W[shard(k, s)], cot[:, n * 256 : (n + 1) * 256])
            for h in range(2):
                total = None
                for t, (di, dj) in enumerate(TAPS):
                    v = moved(SP[t * CS : (t + 1) * CS, h * LT : (h + 1) * LT], -di, -dj)
                    total = v if total is None else total + v
                use(cols(2 * n + h), total)

    def take_first(s):
        ready(0, s)
        for part in range(2):
            patches(lambda at: L[part, rows_of(s), at], part * RS)
            H[part] += tn(W[shard(0, s)], held(part * RS))

    def take_second(s):
        ready(1, s)

        def chain(at, inner):
            SI[pl.ds(al(I0 + s * CS), CS), at] = inner

        spread_back(1, s, GT.at[0], chain)

        def real(at, inner):
            hid = H[1, rows_of(s), at] + BC[0, rows_of(s), :]
            HG[1, rows_of(s), at] = (inner * slope(hid)).astype(BF16)
            UP[1, rows_of(s), at] = leak(hid).astype(BF16)

        spread_back(1, s, GT.at[1], real)

    def turns(q, take):
        @pl.when((q >= 0) & (q < 12))
        def _():
            n, part = lax.div(jnp.maximum(q, 0), 3), lax.rem(jnp.maximum(q, 0), 3)

            def one(u, carry):
                side, flip = lax.rem(u, 2), lax.div(u, 2)
                zz = z + (2 * side - 1) * n
                yy = y + flip - 2 * y * flip

                @pl.when((zz >= 0) & (zz <= 3) & ((n > 0) | (side == 0)))
                def _():
                    take(zz * 2 + yy)

                return carry

            lax.fori_loop(part, part + 1 + lax.div(part, 2), one, 0)

    def slot(r, carry):
        events(0, r)
        events(1, r - 12)
        turns(r - LAG_T, take_first)
        turns(r - 12 - LAG_T, take_second)
        return carry

    lax.fori_loop(4, 24 + LAG_T, slot, 0)

    def tile(n):
        return slice(n * 256, (n + 1) * 256)

    def half_tiles(n):
        return [(h, cols(2 * n + h), cols(h)) for h in range(2)]

    def shard_rows(s, base=0):
        return slice(base + s * CS, base + (s + 1) * CS)

    def step_state(k, n):
        for s in range(NW):
            rows = shard_rows(s)
            for h, at, to in half_tiles(n):
                state = SI[shard_rows(s, S0), at]
                pull = GT[0, rows, at].astype(F32) + slope(state) * H[0, rows, at]
                state = state - pull + 0.01 * NT[k, rows, at].astype(F32)
                SI[shard_rows(s, S0), at] = state
                low = leak(state).astype(BF16)
                L[0, rows, at] = low
                for t, (di, dj) in enumerate(TAPS):
                    PB[n, s * RS + t * CS : s * RS + (t + 1) * CS, to] = moved(low, di, dj)

    def hidden_grad(n, sign, last, patch):
        for s in range(NW):
            rows = shard_rows(s)
            for h, at, to in half_tiles(n):
                hid = H[0, rows, at] + BC[0, rows, :]
                grad = SI[shard_rows(s, I0), at] * slope(hid)
                grad = (grad if sign is None else grad * sign).astype(BF16)
                HG[0, rows, at] = grad
                if last:
                    UP[0, rows, at] = leak(hid).astype(BF16)
                if patch:
                    for t, (di, dj) in enumerate(TAPS):
                        PB[n, t * C + s * CS : t * C + (s + 1) * CS, to] = moved(grad, -di, -dj)

    def product_first(n):
        total = None
        for at in range(0, NW * RS, 2 * C):
            rows = slice(at, min(at + 2 * C, NW * RS))
            part = tn(W[rows, :], PB[n, rows, :])
            total = part if total is None else total + part
        H[0, :, tile(n)] = total

    def product_back(n):
        total = None
        for t in range(0, 9, 2):
            left = jnp.concatenate(
                [
                    jnp.concatenate([W[s * RS + u * CS : s * RS + (u + 1) * CS, :] for s in range(NW)], axis=0)
                    for u in range(t, min(t + 2, 9))
                ],
                axis=1,
            )
            part = nn(left, PB[n, t * C : min(t + 2, 9) * C, :])
            total = part if total is None else total + part
        H[0, :, tile(n)] = total

    hidden_grad(0, None, False, True)

    def langevin(k, carry):
        hidden_grad(1, None, False, True)
        product_back(0)
        hidden_grad(2, None, False, True)
        product_back(1)
        step_state(k, 0)
        product_back(2)
        step_state(k, 1)
        product_first(0)
        step_state(k, 2)
        product_first(1)
        hidden_grad(0, (1 - 2 * k).astype(F32), True, True)
        product_first(2)
        return carry

    lax.fori_loop(0, 2, langevin, 0)
    hidden_grad(1, -1.0, True, False)
    hidden_grad(2, -1.0, True, False)
    for n in range(PX // LT):
        GT[0, :, cols(n)] = -GT[0, :, cols(n)]
    OUT[...] = SI[S0 : S0 + C, :].T

    def out_copy(ref, rows=PX):
        return pltpu.make_async_copy(OUT.at[0:rows], ref, out_sem)

    out_copy(o_fs).start()

    def bias_terms():
        ones = jnp.ones((8, PX), BF16)
        BG[0, 0:8, :] = nt(ones, HG[0]) + nt(ones, HG[1])
        BG[0, 8:16, :] = nt(ones, GT[0]) + nt(ones, GT[1])

    def bg_send(src, dst, sem, dev):
        return pltpu.make_async_remote_copy(
            src_ref=BG.at[src], dst_ref=BG.at[dst], send_sem=bgs_sem.at[sem], recv_sem=bgr_sem.at[sem],
            device_id=dev, device_id_type=MESH,
        )

    def bg_step(i):
        @pl.when(i == 9)
        def _():
            bias_terms()
            bg_send(0, 3, 0, d_sib).start()

        @pl.when(i == 10)
        def _():
            bg_send(0, 3, 0, d_sib).wait()
            BG[1] = BG[0] + BG[3]
            bg_send(1, 4, 1, d_x).start()

        @pl.when(i == 12)
        def _():
            bg_send(1, 4, 1, d_x).wait()
            BG[2] = BG[1] + BG[4]
            bg_send(2, 5, 2, d_y).start()

        @pl.when(i == 14)
        def _():
            bg_send(2, 5, 2, d_y).wait()
            BG[6 + z] = BG[2] + BG[5]
            for by in range(1, 4):
                bg_send(6 + z, 6 + z, 2 + by, (dp, ring_z(by) * 2 + y)).start()

        @pl.when(i == 17)
        def _():
            for by in range(1, 4):
                bg_send(6 + z, 6 + z, 2 + by, (dp, ring_z(by) * 2 + y)).wait()
            BG[0] = BG[6] + BG[7] + BG[8] + BG[9]
            pltpu.make_async_copy(BG.at[0], o_b, own_sem.at[3]).start()

    def shard_of(a):
        p = lax.rem(a, 8)
        flips = 3 - lax.div(p, 2)
        zz = 2 * lax.rem(z_hi + lax.div(flips, 2), 2) + lax.rem(z_lo + lax.rem(flips, 2), 2)
        yy = lax.rem(y + 1 + lax.rem(p, 2), 2)
        return zz, yy

    def both_held():
        return jnp.concatenate([held(0), held(RS)], axis=1)

    def first_block(s, buf):
        for part in range(2):
            patches(lambda at: L[part, rows_of(s), at], part * RS)
        G[buf] = nt(both_held(), jnp.concatenate([HG[0], HG[1]], axis=1))

    def second_block(s, buf):
        for part in range(2):
            patches(lambda at: UP[part, rows_of(s), at], part * RS)
        G[buf] = nt(both_held(), jnp.concatenate([GT[0], GT[1]], axis=1))

    def real_piece(p, carry):
        @pl.when(p < 8)
        def _():
            patches(lambda at: UP[1, rows_of(p), at], 2 * RS)
            add = tn(W[shard(1, p)], held(2 * RS))

            @pl.when(p == 0)
            def _():
                H[0] = add

            @pl.when(p > 0)
            def _():
                H[0] += add

        @pl.when(p >= 8)
        def _():
            s = p - 8

            def keep(at, total):
                H[1, rows_of(s), at] = total

            spread_back(0, s, HG.at[1], keep)

        return carry

    def real_pieces(i):
        def done(at):
            return jnp.minimum(jnp.clip(at - FILL, 0, 8) + jnp.clip(at - TAIL, 0, 8) + 2 * jnp.clip(at - 20, 0, 4), 16)

        lax.fori_loop(done(i), done(i + 1), real_piece, 0)

    def remote(src, dst, ss, rs, dev):
        return pltpu.make_async_remote_copy(
            src_ref=src, dst_ref=dst, send_sem=ss, recv_sem=rs, device_id=dev, device_id_type=MESH
        )

    def core_send(a, core):
        h = lax.rem(a, 2)
        rows = 2 * GR if core == 0 else GR
        return remote(CSB.at[h, 0:rows], CR.at[h, 0:rows], cs_sem.at[h], cr_sem.at[h], d_sib)

    def tap(j):
        return slice(j * CS, (j + 1) * CS)

    def x_out(h, j):
        return lax.div(h, 2), pl.ds(al(lax.rem(h, 2) * GR + j * CS), CS), slice(0, C)

    def x_send(a, j):
        q, h = lax.rem(a, XSLOTS), lax.rem(a, 4)
        return remote(NT.at[x_out(h, j)], XRV.at[q, tap(j)], xs_sem.at[h, j], xr_sem.at[q, j], d_x)

    def y_send(a, zz, j):
        q = lax.rem(lax.div(a, 2), 2)
        return remote(YSB.at[q, tap(j)], YR.at[zz, tap(j)], ys_sem.at[q, j], yr_sem.at[zz, j], d_y)

    def z_send(a, pair, j):
        q = lax.rem(lax.div(a, 2), 2)
        land = XIN.at[lax.div(a, 8), pair * GR + j * CS : pair * GR + (j + 1) * CS, :]
        return remote(
            ZSB.at[q, tap(j)], land, zs_sem.at[q, j], zr_sem.at[lax.div(a, 8), pair, j], d_z2 if pair == 1 else d_z1
        )

    def f_send(turn_, j):
        return remote(FSB.at[tap(j)], FXR.at[turn_, tap(j)], fs_sem.at[turn_, j], fr_sem.at[turn_, j], d_x)

    def f2_send(turn_, src, row, j, n):
        to = FCR.at[pl.ds(al(row + j * CS), CS)]
        return remote(src.at[tap(j)], to, f2s_sem.at[turn_, n, j], f2r_sem.at[turn_, n, j], d_sib)

    def acc(a, j):
        half, odd = lax.div(a, 2), lax.rem(a, 2)
        slot_ = lax.rem(half, 2) * (1 - odd) + (2 + lax.rem(half, 3)) * odd
        return pl.ds(al(slot_ * GR + j * CS), CS)

    def reduce_step(i, carry):
        @pl.when((i >= LAG_C) & (i < 16 + LAG_C))
        def _():
            a = i - LAG_C
            zz, yy = shard_of(a)
            q = lax.rem(lax.div(a, 2), 2)
            for j in range(3):

                @pl.when(c == 1)
                def _(j=j):
                    x_send(a, j).wait_recv()
                    SI[acc(a, j), 0:C] += XRV[lax.rem(a, XSLOTS), tap(j)].astype(F32)

                @pl.when(lax.rem(a, 2) == 0)
                def _(j=j):
                    @pl.when(a >= 4)
                    def _():
                        y_send(a - 4, 0, j).wait_send()

                    YSB[q, tap(j)] = SI[acc(a, j), 0:C].astype(BF16)
                    y_send(a, zz, j).start()

        @pl.when(i < 16)
        def _():
            zz, yy = shard_of(i)
            s = zz * 2 + yy
            buf = lax.rem(i, 2)

            @pl.when(i < 8)
            def _():
                second_block(s, buf)

            @pl.when(i >= 8)
            def _():
                first_block(s, buf)

        @pl.when((i >= 1) & (i < 17))
        def _():
            a = i - 1
            q, h, buf = lax.rem(a, 2), lax.rem(a, 4), lax.rem(a, 2)

            @pl.when(c == 0)
            def _():
                core_send(a, 1).wait_recv()
                for j in range(3):
                    SI[acc(a, j), 0:C] = G[buf, tap(j), :] + CR[q, tap(j), :].astype(F32)

            @pl.when(c == 1)
            def _():
                core_send(a, 0).wait_recv()

                def theirs(g, j):
                    return (
                        G[buf, pl.ds(al(g * GR + j * CS), CS), :]
                        + CR[q, pl.ds(al(jnp.maximum(g - 1, 0) * GR + j * CS), CS), :].astype(F32)
                    )

                for j in range(3):

                    @pl.when(a >= 4)
                    def _(j=j):
                        x_send(a - 4, j).wait_send()

                    NT[x_out(h, j)] = theirs(oth_g, j).astype(BF16)
                    x_send(a, j).start()
                for j in range(3):
                    SI[acc(a, j), 0:C] = theirs(own_g, j)

        @pl.when(i < 16)
        def _():
            buf, h = lax.rem(i, 2), lax.rem(i, 2)

            for core in range(2):

                @pl.when(c == core)
                def _(core=core):
                    @pl.when(i >= 2)
                    def _():
                        core_send(i - 2, core).wait_send()

                    if core == 0:
                        CSB[h] = G[buf, GR : 3 * GR, :].astype(BF16)
                    else:
                        CSB[h, 0:GR] = G[buf, 0:GR, :].astype(BF16)
                    core_send(i, core).start()

        @pl.when((i >= LAG_D + 1) & (i < 16 + LAG_D) & (lax.rem(i + LAG_D, 2) == 1))
        def _():
            a = i - LAG_D
            zz, yy = shard_of(a)
            pair = lax.div(lax.rem(a, 8), 2)
            q, turn_ = lax.rem(lax.div(a, 2), 2), lax.div(a, 8)
            for j in range(3):
                y_send(a, zz, j).wait_recv()
                total = SI[acc(a, j), 0:C] + YR[zz, tap(j)].astype(F32)

                def met(pair_, j=j):
                    z_send(a, pair_, j).wait_recv()
                    at = slice(pair_ * GR + j * CS, pair_ * GR + (j + 1) * CS)
                    return XIN[turn_, at, :].astype(F32)

                @pl.when(pair < 3)
                def _(j=j):
                    @pl.when(a >= 5)
                    def _():
                        z_send(a, 0, j).wait_send()

                for pair_ in range(3):

                    @pl.when(pair == pair_)
                    def _(pair_=pair_, j=j, total=total, met=met):
                        whole = total + met(0) if pair_ == 1 else total
                        ZSB[q, tap(j)] = whole.astype(BF16)
                        z_send(a, pair_, j).start()

                @pl.when(pair == 3)
                def _(j=j, total=total, met=met):
                    FSB[tap(j)] = (total + met(1) + met(2)).astype(BF16)
                    f_send(turn_, j).start()

        for turn_, ref in ((0, o_g2), (1, o_g1)):
            base = 8 * turn_

            @pl.when(i == base + F2)
            def _(turn_=turn_):
                for j in range(3):
                    f_send(turn_, j).wait()

                    @pl.when(c == 0)
                    def _(j=j):
                        both = FSB[tap(j)].astype(F32) + FXR[turn_, tap(j)].astype(F32)
                        FSB[tap(j)] = both.astype(BF16)
                        f2_send(turn_, FSB, 0, j, 0).start()

                    @pl.when(c == 1)
                    def _(j=j):
                        f2_send(turn_, FSB, (own_g - 1) * GR, j, own_g - 1).start()
                        f2_send(turn_, FXR.at[turn_], (oth_g - 1) * GR, j, oth_g - 1).start()

            @pl.when(i == base + F3)
            def _(turn_=turn_, ref=ref):
                out_copy(o_fs).wait()

                @pl.when(c == 0)
                def _():
                    for j in range(3):
                        OUT[tap(j), :] = FSB[tap(j)].astype(F32)
                    for n in range(2):
                        for j in range(3):
                            f2_send(turn_, FSB, n * GR, j, n).wait_recv()
                            at = slice(n * GR + j * CS, n * GR + (j + 1) * CS)
                            OUT[GR + n * GR + j * CS : GR + n * GR + (j + 1) * CS, :] = FCR[at].astype(F32)
                    for j in range(3):
                        f2_send(turn_, FSB, 0, j, 0).wait_send()

                @pl.when(c == 1)
                def _():
                    OUT[pl.ds(al(jnp.maximum(own_g, 1) * GR), GR), :] = FSB[...].astype(F32)
                    OUT[pl.ds(al(jnp.maximum(oth_g, 1) * GR), GR), :] = FXR[turn_].astype(F32)
                    for j in range(3):
                        f2_send(turn_, FSB, 0, j, 0).wait_recv()
                        OUT[tap(j), :] = FCR[tap(j)].astype(F32)
                    for j in range(3):
                        f2_send(turn_, FSB, 0, j, own_g - 1).wait_send()
                        f2_send(turn_, FXR.at[turn_], 0, j, oth_g - 1).wait_send()

                out_copy(ref, RS).start()

        real_pieces(i)

        @pl.when(i == F3 + 1)
        def _():
            out_copy(o_g2, RS).wait()
            for n in range(PX // LT):
                whole = XRT[:, cols(n)].astype(F32) + H[0, :, cols(n)] + BC[1]
                OUT[n * LT : (n + 1) * LT, :] = whole.T
            out_copy(o_blk).start()

        @pl.when(i == 8 + F2)
        def _():
            out_copy(o_blk).wait()
            for n in range(PX // LT):
                whole = GT[1, :, cols(n)].astype(F32) + slope(XRT[:, cols(n)].astype(F32)) * H[1, :, cols(n)]
                OUT[n * LT : (n + 1) * LT, :] = whole.T
            out_copy(o_ig).start()

        bg_step(i)
        return carry

    lax.fori_loop(0, 8 + F3 + 1, reduce_step, 0)

    out_copy(o_g1, RS).wait()
    pltpu.make_async_copy(BG.at[0], o_b, own_sem.at[3]).wait()
    for by in range(1, NW):
        bias_message(by).wait_send()

    def drain(way, planes, rows):
        part = W.at[0 : planes * rows]
        remote(part, part, g_ssem.at[way], g_rsem.at[0, 0, 0], d_sib).wait_send()

    for zz in range(4):

        @pl.when(z == zz)
        def _(zz=zz):
            if zz < 3:
                drain(RIGHT, 2 * (zz + 1), GR)
            if zz > 0:
                drain(LEFT, 2 * (4 - zz), GR)

    drain(YN, 8, GR)

    @pl.when(c == 0)
    def _():
        drain(SIB, 14, GR)
        for a in range(14, 16):
            core_send(a, 0).wait_send()

    @pl.when(c == 1)
    def _():
        drain(SIB, 14, 2 * GR)
        drain(XN, 14, GR)
        for a in range(14, 16):
            core_send(a, 1).wait_send()
        for a in range(12, 16):
            for j in range(3):
                x_send(a, j).wait_send()

    for j in range(3):
        for a in (12, 14):
            y_send(a, 0, j).wait_send()
        for a in (11, 13):
            z_send(a, 0, j).wait_send()


PIECES = 3


def hand_over(blk, ig, fs, g1, g2, bsum, o_blk, o_ig, o_fs, o_g1, o_g2, o_b1, o_b2, wide, tall, sem):
    loads, stores = [], []
    for n, (src, dst) in enumerate(((blk, o_blk), (ig, o_ig), (fs, o_fs), (g1, o_g1), (g2, o_g2))):
        rows = src.shape[0] // PIECES
        for p in range(PIECES):
            at = pl.ds(p * rows, rows)
            held = wide.at[n, at] if n < 3 else tall.at[n - 3, at]
            loads.append(pltpu.make_async_copy(src.at[at], held, sem.at[0, n, p]))
            stores.append(pltpu.make_async_copy(held, dst.at[at], sem.at[1, n, p]))
            loads[-1].start()
    w = lax.axis_index("wide")
    for s in range(NW):

        @pl.when(w == s)
        def _(s=s):
            o_b1[...] = bsum[0:1, s * CS : (s + 1) * CS]
            o_b2[...] = bsum[8:9, s * CS : (s + 1) * CS]

    for load, store in zip(loads, stores):
        load.wait()
        store.start()
    for store in stores:
        store.wait()


def kernel_local(real_images, replay_chains, langevin_noise, real_cot, chain_cot, kernel_one, bias_one, kernel_two, bias_two):
    def flat(values):
        return values.reshape(values.shape[:-4] + (PX, C))

    anywhere = pl.BlockSpec(memory_space=pl.ANY)
    dma = pltpu.SemaphoreType.DMA
    out_shape = [jax.ShapeDtypeStruct((PX, C), F32)] * 3 + [jax.ShapeDtypeStruct((RS, C), F32)] * 2
    out_shape += [jax.ShapeDtypeStruct((16, C), F32)]
    scratch = [
        pltpu.VMEM((2 * NW * RS, C), BF16),
        pltpu.VMEM((2, PX, C), BF16),
        pltpu.VMEM((2, C, PX), BF16),
        pltpu.VMEM((2, C, PX), BF16),
        pltpu.VMEM((C, PX), BF16),
        pltpu.VMEM((2, C, PX), BF16),
        pltpu.VMEM((2 * C, PX), F32),
        pltpu.VMEM((2, C, PX), F32),
        pltpu.VMEM((2, C, PX), BF16),
        pltpu.VMEM((2, C, PX), BF16),
        pltpu.VMEM((PX // 256, NW * RS, 256), BF16),
        pltpu.VMEM((RS, 256), F32),
        pltpu.VMEM((2, RS, C), F32),
        pltpu.VMEM((PX, C), F32),
        pltpu.VMEM((2, C, LT), F32),
        pltpu.VMEM((NW, 8, LT), F32),
        pltpu.VMEM((10, 16, C), F32),
        pltpu.VMEM((2, 2 * GR, C), BF16),
        pltpu.VMEM((XSLOTS, GR, C), BF16),
        pltpu.VMEM((4, GR, C), BF16),
        pltpu.VMEM((2, GR, C), BF16),
        pltpu.VMEM((2 * GR, C), BF16),
        pltpu.VMEM((2, 2 * GR, C), BF16),
        pltpu.VMEM((2, GR, C), BF16),
        pltpu.VMEM((2, GR, C), BF16),
        pltpu.VMEM((GR, C), BF16),
        dma((2,)), dma((4,)), dma, dma((NW,)), dma((NW,)), dma((5,)), dma((2, NW, 9)),
        dma((2,)), dma((2,)), dma((4, 3)), dma((XSLOTS, 3)), dma((2, 3)), dma((4, 3)), dma((2, 3)), dma((2, 3, 3)),
        dma((2, 3)), dma((2, 3)), dma((2, 2, 3)), dma((2, 2, 3)), dma((6,)), dma((6,)),
    ]
    made = pl.pallas_call(
        body,
        out_shape=out_shape,
        in_specs=[anywhere] * 7 + [pl.BlockSpec(memory_space=pltpu.VMEM)] * 2,
        out_specs=[anywhere] * 6,
        scratch_shapes=scratch,
        compiler_params=pltpu.CompilerParams(
            collective_id=0, has_side_effects=True, vmem_limit_bytes=65400 * 2**10
        ),
    )(
        flat(real_images), flat(replay_chains), flat(langevin_noise), flat(real_cot), flat(chain_cot),
        kernel_one.reshape(RS, C), kernel_two.reshape(RS, C), bias_one.reshape(1, CS), bias_two.reshape(1, CS),
    )
    blk, ig, fs, g1, g2, first_bias, second_bias = pl.pallas_call(
        hand_over,
        out_shape=out_shape[:5] + [jax.ShapeDtypeStruct((1, CS), F32)] * 2,
        in_specs=[anywhere] * 5 + [pl.BlockSpec(memory_space=pltpu.VMEM)],
        out_specs=[anywhere] * 5 + [pl.BlockSpec(memory_space=pltpu.VMEM)] * 2,
        scratch_shapes=[pltpu.VMEM((3, PX, C), F32), pltpu.VMEM((2, RS, C), F32), dma((2, 5, PIECES))],
    )(*made)
    shape = real_images.shape
    return (
        blk.reshape(shape), ig.reshape(shape), fs.reshape(shape),
        g1.reshape(kernel_one.shape), first_bias.reshape(CS),
        g2.reshape(kernel_two.shape), second_bias.reshape(CS),
    )


def solution(mesh):
    def local(real_images, *rest):
        kernel_one = rest[4]
        fits = (
            mesh.shape["dp"] == 4
            and mesh.shape["wide"] == NW
            and real_images.shape == (12, 8, 8, C)
            and kernel_one.shape == (3, 3, CS, C)
            and rest[1].shape[0] == 2
        )
        return (kernel_local if fits else plain_local)(real_images, *rest)

    return jax.shard_map(
        local,
        mesh=mesh,
        in_specs=(
            P(("dp", "wide"), None, None, None),
            P(("dp", "wide"), None, None, None),
            P(None, ("dp", "wide"), None, None, None),
            P(("dp", "wide"), None, None, None),
            P(("dp", "wide"), None, None, None),
            P(None, None, "wide", None),
            P("wide"),
            P(None, None, "wide", None),
            P("wide"),
        ),
        out_specs=(
            P(("dp", "wide"), None, None, None),
            P(("dp", "wide"), None, None, None),
            P(("dp", "wide"), None, None, None),
            P(None, None, "wide", None),
            P("wide"),
            P(None, None, "wide", None),
            P("wide"),
        ),
        check_vma=False,
    )
```

```python
import functools

import jax
import jax.numpy as jnp
from jax import lax
from jax.experimental import pallas as pl
from jax.experimental.pallas import tpu as pltpu
from jax.sharding import PartitionSpec as P

F32 = jnp.float32
BF16 = jnp.bfloat16
MESH = pl.DeviceIdType.MESH


def leaky_relu(values):
    return jnp.where(values > 0, values, 0.2 * values)


def leak_slope(values):
    return jnp.where(values > 0, 1.0, 0.2).astype(F32)


def tap_patches(activation):
    batch_size, height, map_width, channels = activation.shape
    padded = jnp.pad(activation, ((0, 0), (1, 1), (1, 1), (0, 0)))
    tap_list = [
        padded[:, row_off : row_off + height, col_off : col_off + map_width, :]
        for row_off in range(3)
        for col_off in range(3)
    ]
    return jnp.stack(tap_list, axis=3).reshape(batch_size * height * map_width, 9 * channels)


def conv_apply(activation, kernel_mat, bias_row):
    result = jnp.dot(tap_patches(activation), kernel_mat, preferred_element_type=F32)
    return result.reshape(activation.shape[:3] + (kernel_mat.shape[1],)) + bias_row.astype(F32)


def conv_back(gradient, kernel_mat):
    batch_size, height, map_width, channels = gradient.shape
    in_channels = kernel_mat.shape[0] // 9
    spread = lax.dot_general(
        gradient.reshape(-1, channels), kernel_mat, (((1,), (1,)), ((), ())), preferred_element_type=F32
    )
    spread = spread.reshape(batch_size, height, map_width, 9, in_channels)
    summed = jnp.zeros((batch_size, height + 2, map_width + 2, in_channels), F32)
    for row_off in range(3):
        for col_off in range(3):
            summed = summed + jnp.pad(
                spread[:, :, :, 3 * row_off + col_off, :],
                ((0, 0), (row_off, 2 - row_off), (col_off, 2 - col_off), (0, 0)),
            )
    return summed[:, 1 : height + 1, 1 : map_width + 1, :]


def kernel_partial(activation, gradient):
    channels = gradient.shape[3]
    return lax.dot_general(
        tap_patches(activation),
        gradient.reshape(-1, channels),
        (((0,), (0,)), ((), ())),
        preferred_element_type=F32,
    )


def plain_local(real_images, replay_chains, langevin_noise, real_cot, chain_cot, kernel_one, bias_one, kernel_two, bias_two):
    def whole(kernel):
        gathered = lax.all_gather(kernel, "wide", axis=2, tiled=True)
        return gathered.reshape(9 * gathered.shape[2], gathered.shape[3])

    first, second = whole(kernel_one), whole(kernel_two)
    first_bias = lax.all_gather(bias_one, "wide", axis=0, tiled=True)
    second_bias = lax.all_gather(bias_two, "wide", axis=0, tiled=True)

    def hidden_of(values):
        lower = leaky_relu(values).astype(BF16)
        return lower, conv_apply(lower, first, first_bias)

    def x_grad(values, cot, hidden_grad):
        return cot.astype(F32) + leak_slope(values) * conv_back(hidden_grad, first)

    chain_inner = conv_back(chain_cot, second)
    state = replay_chains.astype(F32)
    for step_index in range(langevin_noise.shape[0]):
        _, hidden = hidden_of(state)
        hidden_grad = (chain_inner * leak_slope(hidden)).astype(BF16)
        state = state - x_grad(state, chain_cot, hidden_grad) + 0.01 * langevin_noise[step_index].astype(F32)
    real = real_images.astype(F32)
    real_lower, real_hidden = hidden_of(real)
    real_upper = leaky_relu(real_hidden).astype(BF16)
    block_output = real + conv_apply(real_upper, second, second_bias)
    sample_lower, sample_hidden = hidden_of(state)
    sample_upper = leaky_relu(sample_hidden).astype(BF16)
    real_hgrad = (conv_back(real_cot, second) * leak_slope(real_hidden)).astype(BF16)
    input_grad = x_grad(real, real_cot, real_hgrad)
    sample_hgrad = -((chain_inner * leak_slope(sample_hidden)).astype(BF16))

    def bias_sum(values):
        return jnp.sum(values.astype(F32), axis=(0, 1, 2))

    totals = (
        kernel_partial(real_lower, real_hgrad) + kernel_partial(sample_lower, sample_hgrad),
        bias_sum(real_hgrad) + bias_sum(sample_hgrad),
        kernel_partial(real_upper, real_cot) + kernel_partial(sample_upper, -chain_cot),
        bias_sum(real_cot) - bias_sum(chain_cot),
    )
    channels = kernel_one.shape[3]
    kernel_shape = (3, 3, channels, channels)
    shares = (
        lax.psum_scatter(totals[0].reshape(kernel_shape), "wide", scatter_dimension=2, tiled=True),
        lax.psum_scatter(totals[1], "wide", scatter_dimension=0, tiled=True),
        lax.psum_scatter(totals[2].reshape(kernel_shape), "wide", scatter_dimension=2, tiled=True),
        lax.psum_scatter(totals[3], "wide", scatter_dimension=0, tiled=True),
    )
    summed = lax.psum(shares, "dp")
    return (block_output, input_grad, state, summed[0], summed[1], summed[2], summed[3])


NW = 8
C = 640
CS = C // NW
PX = 768
RS = 9 * CS
GR = 3 * CS
LT = 128
TAPS = [(p - 1, q - 1) for p in range(3) for q in range(3)]

LAG_C, LAG_D = 3, 5
XSLOTS = 2 * LAG_C - 2
F2 = 8 + LAG_D
F3 = F2 + 1

RIGHT, LEFT, YN, SIB, XN = range(5)
LAG_Y, LAG_X = 4, 4
LAG_T = LAG_Y + LAG_X


def tn(a, b):
    return lax.dot_general(a, b, (((0,), (0,)), ((), ())), preferred_element_type=F32)


def nt(a, b):
    return lax.dot_general(a, b, (((1,), (1,)), ((), ())), preferred_element_type=F32)


def nn(a, b):
    return jnp.dot(a, b, preferred_element_type=F32)


def leak(v):
    return jnp.where(v > 0, v, 0.2 * v)


def slope(v):
    return jnp.where(v > 0, 1.0, 0.2).astype(F32)


def inside(di, dj):
    lane = lax.broadcasted_iota(jnp.int32, (1, LT), 1)
    row, col = (lane // 8) % 8 + di, lane % 8 + dj
    return (row >= 0) & (row < 8) & (col >= 0) & (col < 8)


def turn(v, by):
    by %= LT
    return v if by == 0 else pltpu.roll(v, by, 1)


def moved(v, di, dj):
    if di == 0 and dj == 0:
        return v
    return jnp.where(inside(di, dj), turn(v, -(8 * di + dj)), jnp.zeros_like(v))


def al(row, by=16):
    return pl.multiple_of(row, by)


def body(
    xr, xc, nz, gr, gc, k1, k2, b1, b2,
    o_blk, o_ig, o_fs, o_g1, o_g2, o_b,
    W, XIN, GT, NT, XRT, L, SI, H, HG, UP, PB, SP, G, OUT, BC, BT, BG,
    CR, XRV, YR, FXR, FCR, CSB, YSB, ZSB, FSB,
    in_sem, own_sem, out_sem, b_ssem, b_rsem, g_ssem, g_rsem,
    cs_sem, cr_sem, xs_sem, xr_sem, ys_sem, yr_sem, zs_sem, zr_sem, fs_sem, fr_sem, f2s_sem, f2r_sem,
    bgs_sem, bgr_sem,
):
    dp, w = lax.axis_index("dp"), lax.axis_index("wide")
    x, c = lax.div(dp, 2), lax.rem(dp, 2)
    z, y = lax.div(w, 2), lax.rem(w, 2)
    d_sib = (x * 2 + 1 - c, w)
    d_x = ((1 - x) * 2 + c, w)
    d_y = (dp, z * 2 + 1 - y)
    z_hi, z_lo = lax.div(z, 2), lax.rem(z, 2)
    d_z1 = (dp, (2 * z_hi + 1 - z_lo) * 2 + y)
    d_z2 = (dp, (2 * (1 - z_hi) + z_lo) * 2 + y)
    d_right = (dp, w + 2)
    d_left = (dp, w - 2)
    own_g = c * (1 + x)
    oth_g = c * (2 - x)

    def ring_z(by):
        return lax.rem(z + by, 4)

    barrier = pltpu.get_barrier_semaphore()
    greeted = [d_sib, d_x] + [(dp, lax.rem(w + by, NW)) for by in range(1, NW)]
    for dev in greeted:
        pl.semaphore_signal(barrier, inc=1, device_id=dev, device_id_type=MESH)

    def shard(k, s):
        return pl.ds(al((k * NW + s) * RS), RS)

    def own_copy(k):
        return pltpu.make_async_copy((k1, k2)[k], W.at[shard(k, w)], own_sem.at[k])

    own_copy(0).start()
    own_copy(1).start()
    BT[w] = jnp.zeros((8, LT), F32)
    BT[w, 0:1, 0:CS] = b1[...].astype(F32)
    BT[w, 1:2, 0:CS] = b2[...].astype(F32)
    sources = [xc, xr, gc, gr, nz.at[0], nz.at[1]]

    def in_copy(n):
        return pltpu.make_async_copy(sources[n], XIN.at[n % 2], in_sem.at[n % 2])

    in_copy(0).start()
    in_copy(1).start()
    own_copy(0).wait()
    own_copy(1).wait()
    pl.semaphore_wait(barrier, len(greeted))

    devs = {RIGHT: d_right, LEFT: d_left, YN: d_y, SIB: d_sib, XN: d_x}

    def message(k, s, tap, way):
        part = W.at[pl.ds(al((k * NW + s) * RS + tap * CS), CS)]
        return pltpu.make_async_remote_copy(
            src_ref=part, dst_ref=part, send_sem=g_ssem.at[way], recv_sem=g_rsem.at[k, s, tap],
            device_id=devs[way], device_id_type=MESH,
        )

    def arrive(k, s, tap):
        message(k, s, tap, YN).wait_recv()

    def by_z(k, j):
        return (j == 2) & (k == 1)

    def events(k, m):
        def z_part(n, j):
            tap = own_g * 3 + j

            @pl.when(n == 0)
            def _():
                @pl.when(z < 3)
                def _():
                    message(k, w, tap, RIGHT).start()

                @pl.when(z > 0)
                def _():
                    message(k, w, tap, LEFT).start()

                message(k, w, tap, YN).start()

            def flow(zz, onward, may):
                s = zz * 2 + y
                arrive(k, s, tap)

                @pl.when(may)
                def _():
                    message(k, s, tap, onward).start()

                @pl.when(jnp.logical_not(by_z(k, j)))
                def _():
                    message(k, s, tap, YN).start()

                message(k, s, tap, SIB).start()

                @pl.when(c == 1)
                def _():
                    message(k, s, tap, XN).start()

            @pl.when((n >= 1) & (z - n >= 0))
            def _():
                flow(z - n, RIGHT, z < 3)

            @pl.when((n >= 1) & (z + n <= 3))
            def _():
                flow(z + n, LEFT, z > 0)

        def y_part(n, j):
            tap = own_g * 3 + j

            def flow(zz, right, left):
                s = zz * 2 + 1 - y
                arrive(k, s, tap)

                @pl.when(by_z(k, j) & right)
                def _():
                    message(k, s, tap, RIGHT).start()

                @pl.when(by_z(k, j) & left)
                def _():
                    message(k, s, tap, LEFT).start()

                message(k, s, tap, SIB).start()

                @pl.when(c == 1)
                def _():
                    message(k, s, tap, XN).start()

            @pl.when(z - n >= 0)
            def _():
                flow(z - n, z < 3, (n == 0) & (z > 0))

            @pl.when((n >= 1) & (z + n <= 3))
            def _():
                flow(z + n, z < 0, z > 0)

        def x_part(n, j, yy, least):
            tap = oth_g * 3 + j

            def flow(zz):
                s = zz * 2 + yy
                arrive(k, s, tap)
                message(k, s, tap, SIB).start()

            @pl.when((c == 1) & (n >= least) & (z - n >= 0))
            def _():
                flow(z - n)

            @pl.when((c == 1) & (n >= 1) & (z + n <= 3))
            def _():
                flow(z + n)

        for lag, part in (
            (LAG_Y + LAG_X, lambda n, j: x_part(n, j, 1 - y, 0)),
            (LAG_X, lambda n, j: x_part(n, j, y, 1)),
            (LAG_Y, y_part),
            (0, z_part),
        ):
            at = m - lag

            @pl.when((at >= 0) & (at < 12))
            def _(part=part, at=at):
                at = jnp.maximum(at, 0)
                part(lax.div(at, 3), lax.rem(at, 3))

    def ready(k, s):
        @pl.when(s != w)
        def _():
            @pl.when(c == 0)
            def _():
                for tap in range(3, 9):
                    arrive(k, s, tap)

            @pl.when(c == 1)
            def _():
                for tap in range(3):
                    arrive(k, s, tap)

    def bias_message(by):
        return pltpu.make_async_remote_copy(
            src_ref=BT.at[w], dst_ref=BT.at[w], send_sem=b_ssem.at[by], recv_sem=b_rsem.at[w],
            device_id=(dp, lax.rem(w + by, NW)), device_id_type=MESH,
        )

    def bias_arrive(by):
        s = lax.rem(w + by, NW)
        pltpu.make_async_remote_copy(
            src_ref=BT.at[s], dst_ref=BT.at[s], send_sem=b_ssem.at[by], recv_sem=b_rsem.at[s],
            device_id=(dp, s), device_id_type=MESH,
        ).wait_recv()

    events(0, 0)
    for by in range(1, NW):
        bias_message(by).start()

    S0, I0 = 0, C

    for n in range(6):
        in_copy(n).wait()
        if n == 0:
            t = XIN[0].T.astype(F32)
            SI[S0 : S0 + C, :] = t
            L[0] = leak(t).astype(BF16)
        elif n == 1:
            t = XIN[1].T
            XRT[...] = t
            L[1] = leak(t.astype(F32)).astype(BF16)
        elif n < 4:
            GT[n - 2] = XIN[n % 2].T
        else:
            NT[n - 4] = XIN[n % 2].T
        if n + 2 < 6:
            in_copy(n + 2).start()
        events(0, n + 1) if n < 2 else None
    H[...] = jnp.zeros_like(H)
    events(0, 3)
    for by in range(1, NW):
        bias_arrive(by)

    def bias_columns(s, carry):
        for k in range(2):
            row = jnp.broadcast_to(BT[s, k : k + 1, :], (LT, LT))
            BC[k, pl.ds(al(s * CS), CS), :] = row.T[0:CS, :]
        return carry

    lax.fori_loop(0, NW, bias_columns, 0)

    def rows_of(s):
        return pl.ds(al(s * CS), CS)

    def cols(n):
        return slice(n * LT, (n + 1) * LT)

    def patches(load, row):
        for n in range(PX // LT):
            v = load(cols(n))
            for t, (di, dj) in enumerate(TAPS):
                PB[n // 2, row + t * CS : row + (t + 1) * CS, cols(n % 2)] = moved(v, di, dj)

    def held(row):
        return jnp.concatenate([PB[m, row : row + RS, :] for m in range(PX // 256)], axis=1)

    def spread_back(k, s, cot, use):
        for n in range(PX // 256):
            SP[...] = nn(W[shard(k, s)], cot[:, n * 256 : (n + 1) * 256])
            for h in range(2):
                total = None
                for t, (di, dj) in enumerate(TAPS):
                    v = moved(SP[t * CS : (t + 1) * CS, h * LT : (h + 1) * LT], -di, -dj)
                    total = v if total is None else total + v
                use(cols(2 * n + h), total)

    def take_first(s):
        ready(0, s)
        for part in range(2):
            patches(lambda at: L[part, rows_of(s), at], part * RS)
            H[part] += tn(W[shard(0, s)], held(part * RS))

    def take_second(s):
        ready(1, s)

        def chain(at, inner):
            SI[pl.ds(al(I0 + s * CS), CS), at] = inner

        spread_back(1, s, GT.at[0], chain)

        for n in range(PX // LT):
            hid = H[1, rows_of(s), cols(n)] + BC[0, rows_of(s), :]
            UP[1, rows_of(s), cols(n)] = leak(hid).astype(BF16)

    def turns(q, take):
        @pl.when((q >= 0) & (q < 12))
        def _():
            n, part = lax.div(jnp.maximum(q, 0), 3), lax.rem(jnp.maximum(q, 0), 3)

            def one(u, carry):
                side, flip = lax.rem(u, 2), lax.div(u, 2)
                zz = z + (2 * side - 1) * n
                yy = y + flip - 2 * y * flip

                @pl.when((zz >= 0) & (zz <= 3) & ((n > 0) | (side == 0)))
                def _():
                    take(zz * 2 + yy)

                return carry

            lax.fori_loop(part, part + 1 + lax.div(part, 2), one, 0)

    def slot(r, carry):
        events(0, r)
        events(1, r - 12)
        turns(r - LAG_T, take_first)
        turns(r - 12 - LAG_T, take_second)
        return carry

    lax.fori_loop(4, 24 + LAG_T, slot, 0)

    def tile(n):
        return slice(n * 256, (n + 1) * 256)

    def half_tiles(n):
        return [(h, cols(2 * n + h), cols(h)) for h in range(2)]

    def shard_rows(s, base=0):
        return slice(base + s * CS, base + (s + 1) * CS)

    def step_state(k, n):
        for s in range(NW):
            rows = shard_rows(s)
            for h, at, to in half_tiles(n):
                state = SI[shard_rows(s, S0), at]
                pull = GT[0, rows, at].astype(F32) + slope(state) * H[0, rows, at]
                state = state - pull + 0.01 * NT[k, rows, at].astype(F32)
                SI[shard_rows(s, S0), at] = state
                low = leak(state).astype(BF16)
                L[0, rows, at] = low
                for t, (di, dj) in enumerate(TAPS):
                    PB[n, s * RS + t * CS : s * RS + (t + 1) * CS, to] = moved(low, di, dj)

    def hidden_grad(n, sign, last, patch):
        for s in range(NW):
            rows = shard_rows(s)
            for h, at, to in half_tiles(n):
                hid = H[0, rows, at] + BC[0, rows, :]
                grad = SI[shard_rows(s, I0), at] * slope(hid)
                grad = (grad if sign is None else grad * sign).astype(BF16)
                HG[0, rows, at] = grad
                if last:
                    UP[0, rows, at] = leak(hid).astype(BF16)
                if patch:
                    for t, (di, dj) in enumerate(TAPS):
                        PB[n, t * C + s * CS : t * C + (s + 1) * CS, to] = moved(grad, -di, -dj)

    def product_first(n):
        total = None
        for at in range(0, NW * RS, 2 * C):
            rows = slice(at, min(at + 2 * C, NW * RS))
            part = tn(W[rows, :], PB[n, rows, :])
            total = part if total is None else total + part
        H[0, :, tile(n)] = total

    def product_back(n):
        total = None
        for t in range(0, 9, 2):
            left = jnp.concatenate(
                [
                    jnp.concatenate([W[s * RS + u * CS : s * RS + (u + 1) * CS, :] for s in range(NW)], axis=0)
                    for u in range(t, min(t + 2, 9))
                ],
                axis=1,
            )
            part = nn(left, PB[n, t * C : min(t + 2, 9) * C, :])
            total = part if total is None else total + part
        H[0, :, tile(n)] = total

    hidden_grad(0, None, False, True)

    def langevin(k, carry):
        hidden_grad(1, None, False, True)
        product_back(0)
        hidden_grad(2, None, False, True)
        product_back(1)
        step_state(k, 0)
        product_back(2)
        step_state(k, 1)
        product_first(0)
        step_state(k, 2)
        product_first(1)
        hidden_grad(0, (1 - 2 * k).astype(F32), True, True)
        product_first(2)
        return carry

    lax.fori_loop(0, 2, langevin, 0)
    hidden_grad(1, -1.0, True, False)
    hidden_grad(2, -1.0, True, False)
    for n in range(PX // LT):
        GT[0, :, cols(n)] = -GT[0, :, cols(n)]
    OUT[...] = SI[S0 : S0 + C, :].T

    def out_copy(ref, rows=PX):
        return pltpu.make_async_copy(OUT.at[0:rows], ref, out_sem)

    out_copy(o_fs).start()

    def bias_terms():
        ones = jnp.ones((8, PX), BF16)
        BG[0, 0:8, :] = nt(ones, HG[0]) + nt(ones, HG[1])
        BG[0, 8:16, :] = nt(ones, GT[0]) + nt(ones, GT[1])

    def bg_send(src, dst, sem, dev):
        return pltpu.make_async_remote_copy(
            src_ref=BG.at[src], dst_ref=BG.at[dst], send_sem=bgs_sem.at[sem], recv_sem=bgr_sem.at[sem],
            device_id=dev, device_id_type=MESH,
        )

    def bg_step(i):
        @pl.when(i == 9)
        def _():
            bias_terms()
            bg_send(0, 3, 0, d_sib).start()

        @pl.when(i == 10)
        def _():
            bg_send(0, 3, 0, d_sib).wait()
            BG[1] = BG[0] + BG[3]
            bg_send(1, 4, 1, d_x).start()

        @pl.when(i == 12)
        def _():
            bg_send(1, 4, 1, d_x).wait()
            BG[2] = BG[1] + BG[4]
            bg_send(2, 5, 2, d_y).start()

        @pl.when(i == 14)
        def _():
            bg_send(2, 5, 2, d_y).wait()
            BG[6 + z] = BG[2] + BG[5]
            for by in range(1, 4):
                bg_send(6 + z, 6 + z, 2 + by, (dp, ring_z(by) * 2 + y)).start()

        @pl.when(i == 17)
        def _():
            for by in range(1, 4):
                bg_send(6 + z, 6 + z, 2 + by, (dp, ring_z(by) * 2 + y)).wait()
            BG[0] = BG[6] + BG[7] + BG[8] + BG[9]
            pltpu.make_async_copy(BG.at[0], o_b, own_sem.at[3]).start()

    def shard_of(a):
        p = lax.rem(a, 8)
        flips = 3 - lax.div(p, 2)
        zz = 2 * lax.rem(z_hi + lax.div(flips, 2), 2) + lax.rem(z_lo + lax.rem(flips, 2), 2)
        yy = lax.rem(y + 1 + lax.rem(p, 2), 2)
        return zz, yy

    def both_held():
        return jnp.concatenate([held(0), held(RS)], axis=1)

    def first_block(s, buf):
        for part in range(2):
            patches(lambda at: L[part, rows_of(s), at], part * RS)
        G[buf] = nt(both_held(), jnp.concatenate([HG[0], HG[1]], axis=1))

    def second_block(s, buf):
        for part in range(2):
            patches(lambda at: UP[part, rows_of(s), at], part * RS)
        G[buf] = nt(both_held(), jnp.concatenate([GT[0], GT[1]], axis=1))

    def real_piece(p, carry):
        @pl.when(p < 8)
        def _():
            def hidden_of(at, inner):
                hid = H[1, rows_of(p), at] + BC[0, rows_of(p), :]
                HG[1, rows_of(p), at] = (inner * slope(hid)).astype(BF16)

            spread_back(1, p, GT.at[1], hidden_of)

        @pl.when((p >= 8) & (p < 16))
        def _():
            s = p - 8
            patches(lambda at: UP[1, rows_of(s), at], 2 * RS)
            add = tn(W[shard(1, s)], held(2 * RS))

            @pl.when(p == 8)
            def _():
                H[0] = add

            @pl.when(p > 8)
            def _():
                H[0] += add

        @pl.when(p >= 16)
        def _():
            s = p - 16

            def keep(at, total):
                H[1, rows_of(s), at] = total

            spread_back(0, s, HG.at[1], keep)

        return carry

    def real_pieces(i):
        def done(at):
            return jnp.minimum(jnp.clip(at, 0, 16) + jnp.clip(at - 16, 0, 8) + 2 * jnp.clip(at - 20, 0, 4), 24)

        lax.fori_loop(done(i), done(i + 1), real_piece, 0)

    def remote(src, dst, ss, rs, dev):
        return pltpu.make_async_remote_copy(
            src_ref=src, dst_ref=dst, send_sem=ss, recv_sem=rs, device_id=dev, device_id_type=MESH
        )

    def core_send(a, core):
        h = lax.rem(a, 2)
        rows = 2 * GR if core == 0 else GR
        return remote(CSB.at[h, 0:rows], CR.at[h, 0:rows], cs_sem.at[h], cr_sem.at[h], d_sib)

    def tap(j):
        return slice(j * CS, (j + 1) * CS)

    def x_out(h, j):
        return lax.div(h, 2), pl.ds(al(lax.rem(h, 2) * GR + j * CS), CS), slice(0, C)

    def x_send(a, j):
        q, h = lax.rem(a, XSLOTS), lax.rem(a, 4)
        return remote(NT.at[x_out(h, j)], XRV.at[q, tap(j)], xs_sem.at[h, j], xr_sem.at[q, j], d_x)

    def y_send(a, zz, j):
        q = lax.rem(lax.div(a, 2), 2)
        return remote(YSB.at[q, tap(j)], YR.at[zz, tap(j)], ys_sem.at[q, j], yr_sem.at[zz, j], d_y)

    def z_send(a, pair, j):
        q = lax.rem(lax.div(a, 2), 2)
        land = XIN.at[lax.div(a, 8), pair * GR + j * CS : pair * GR + (j + 1) * CS, :]
        return remote(
            ZSB.at[q, tap(j)], land, zs_sem.at[q, j], zr_sem.at[lax.div(a, 8), pair, j], d_z2 if pair == 1 else d_z1
        )

    def f_send(turn_, j):
        return remote(FSB.at[tap(j)], FXR.at[turn_, tap(j)], fs_sem.at[turn_, j], fr_sem.at[turn_, j], d_x)

    def f2_send(turn_, src, row, j, n):
        to = FCR.at[pl.ds(al(row + j * CS), CS)]
        return remote(src.at[tap(j)], to, f2s_sem.at[turn_, n, j], f2r_sem.at[turn_, n, j], d_sib)

    def acc(a, j):
        half, odd = lax.div(a, 2), lax.rem(a, 2)
        slot_ = lax.rem(half, 2) * (1 - odd) + (2 + lax.rem(half, 3)) * odd
        return pl.ds(al(slot_ * GR + j * CS), CS)

    def reduce_step(i, carry):
        @pl.when((i >= LAG_C) & (i < 16 + LAG_C))
        def _():
            a = i - LAG_C
            zz, yy = shard_of(a)
            q = lax.rem(lax.div(a, 2), 2)
            for j in range(3):

                @pl.when(c == 1)
                def _(j=j):
                    x_send(a, j).wait_recv()
                    SI[acc(a, j), 0:C] += XRV[lax.rem(a, XSLOTS), tap(j)].astype(F32)

                @pl.when(lax.rem(a, 2) == 0)
                def _(j=j):
                    @pl.when(a >= 4)
                    def _():
                        y_send(a - 4, 0, j).wait_send()

                    YSB[q, tap(j)] = SI[acc(a, j), 0:C].astype(BF16)
                    y_send(a, zz, j).start()

        @pl.when(i < 16)
        def _():
            zz, yy = shard_of(i)
            s = zz * 2 + yy
            buf = lax.rem(i, 2)

            @pl.when(i < 8)
            def _():
                second_block(s, buf)

            @pl.when(i >= 8)
            def _():
                first_block(s, buf)

        @pl.when((i >= 1) & (i < 17))
        def _():
            a = i - 1
            q, h, buf = lax.rem(a, 2), lax.rem(a, 4), lax.rem(a, 2)

            @pl.when(c == 0)
            def _():
                core_send(a, 1).wait_recv()
                for j in range(3):
                    SI[acc(a, j), 0:C] = G[buf, tap(j), :] + CR[q, tap(j), :].astype(F32)

            @pl.when(c == 1)
            def _():
                core_send(a, 0).wait_recv()

                def theirs(g, j):
                    return (
                        G[buf, pl.ds(al(g * GR + j * CS), CS), :]
                        + CR[q, pl.ds(al(jnp.maximum(g - 1, 0) * GR + j * CS), CS), :].astype(F32)
                    )

                for j in range(3):

                    @pl.when(a >= 4)
                    def _(j=j):
                        x_send(a - 4, j).wait_send()

                    NT[x_out(h, j)] = theirs(oth_g, j).astype(BF16)
                    x_send(a, j).start()
                for j in range(3):
                    SI[acc(a, j), 0:C] = theirs(own_g, j)

        @pl.when(i < 16)
        def _():
            buf, h = lax.rem(i, 2), lax.rem(i, 2)

            for core in range(2):

                @pl.when(c == core)
                def _(core=core):
                    @pl.when(i >= 2)
                    def _():
                        core_send(i - 2, core).wait_send()

                    if core == 0:
                        CSB[h] = G[buf, GR : 3 * GR, :].astype(BF16)
                    else:
                        CSB[h, 0:GR] = G[buf, 0:GR, :].astype(BF16)
                    core_send(i, core).start()

        @pl.when((i >= LAG_D + 1) & (i < 16 + LAG_D) & (lax.rem(i + LAG_D, 2) == 1))
        def _():
            a = i - LAG_D
            zz, yy = shard_of(a)
            pair = lax.div(lax.rem(a, 8), 2)
            q, turn_ = lax.rem(lax.div(a, 2), 2), lax.div(a, 8)
            for j in range(3):
                y_send(a, zz, j).wait_recv()
                total = SI[acc(a, j), 0:C] + YR[zz, tap(j)].astype(F32)

                def met(pair_, j=j):
                    z_send(a, pair_, j).wait_recv()
                    at = slice(pair_ * GR + j * CS, pair_ * GR + (j + 1) * CS)
                    return XIN[turn_, at, :].astype(F32)

                @pl.when(pair < 3)
                def _(j=j):
                    @pl.when(a >= 5)
                    def _():
                        z_send(a, 0, j).wait_send()

                for pair_ in range(3):

                    @pl.when(pair == pair_)
                    def _(pair_=pair_, j=j, total=total, met=met):
                        whole = total + met(0) if pair_ == 1 else total
                        ZSB[q, tap(j)] = whole.astype(BF16)
                        z_send(a, pair_, j).start()

                @pl.when(pair == 3)
                def _(j=j, total=total, met=met):
                    FSB[tap(j)] = (total + met(1) + met(2)).astype(BF16)
                    f_send(turn_, j).start()

        for turn_, ref in ((0, o_g2), (1, o_g1)):
            base = 8 * turn_

            @pl.when(i == base + F2)
            def _(turn_=turn_):
                for j in range(3):
                    f_send(turn_, j).wait()

                    @pl.when(c == 0)
                    def _(j=j):
                        both = FSB[tap(j)].astype(F32) + FXR[turn_, tap(j)].astype(F32)
                        FSB[tap(j)] = both.astype(BF16)
                        f2_send(turn_, FSB, 0, j, 0).start()

                    @pl.when(c == 1)
                    def _(j=j):
                        f2_send(turn_, FSB, (own_g - 1) * GR, j, own_g - 1).start()
                        f2_send(turn_, FXR.at[turn_], (oth_g - 1) * GR, j, oth_g - 1).start()

            @pl.when(i == base + F3)
            def _(turn_=turn_, ref=ref):
                out_copy(o_fs).wait()

                @pl.when(c == 0)
                def _():
                    for j in range(3):
                        OUT[tap(j), :] = FSB[tap(j)].astype(F32)
                    for n in range(2):
                        for j in range(3):
                            f2_send(turn_, FSB, n * GR, j, n).wait_recv()
                            at = slice(n * GR + j * CS, n * GR + (j + 1) * CS)
                            OUT[GR + n * GR + j * CS : GR + n * GR + (j + 1) * CS, :] = FCR[at].astype(F32)
                    for j in range(3):
                        f2_send(turn_, FSB, 0, j, 0).wait_send()

                @pl.when(c == 1)
                def _():
                    OUT[pl.ds(al(jnp.maximum(own_g, 1) * GR), GR), :] = FSB[...].astype(F32)
                    OUT[pl.ds(al(jnp.maximum(oth_g, 1) * GR), GR), :] = FXR[turn_].astype(F32)
                    for j in range(3):
                        f2_send(turn_, FSB, 0, j, 0).wait_recv()
                        OUT[tap(j), :] = FCR[tap(j)].astype(F32)
                    for j in range(3):
                        f2_send(turn_, FSB, 0, j, own_g - 1).wait_send()
                        f2_send(turn_, FXR.at[turn_], 0, j, oth_g - 1).wait_send()

                out_copy(ref, RS).start()

        real_pieces(i)

        @pl.when(i == F3 + 1)
        def _():
            out_copy(o_g2, RS).wait()
            for n in range(PX // LT):
                whole = XRT[:, cols(n)].astype(F32) + H[0, :, cols(n)] + BC[1]
                OUT[n * LT : (n + 1) * LT, :] = whole.T
            out_copy(o_blk).start()

        @pl.when(i == 8 + F2)
        def _():
            out_copy(o_blk).wait()
            for n in range(PX // LT):
                whole = GT[1, :, cols(n)].astype(F32) + slope(XRT[:, cols(n)].astype(F32)) * H[1, :, cols(n)]
                OUT[n * LT : (n + 1) * LT, :] = whole.T
            out_copy(o_ig).start()

        bg_step(i)
        return carry

    lax.fori_loop(0, 8 + F3 + 1, reduce_step, 0)

    out_copy(o_g1, RS).wait()
    pltpu.make_async_copy(BG.at[0], o_b, own_sem.at[3]).wait()
    for by in range(1, NW):
        bias_message(by).wait_send()

    def drain(way, planes, rows):
        part = W.at[0 : planes * rows]
        remote(part, part, g_ssem.at[way], g_rsem.at[0, 0, 0], d_sib).wait_send()

    for zz in range(4):

        @pl.when(z == zz)
        def _(zz=zz):
            if zz < 3:
                drain(RIGHT, zz + 1, 7 * CS)
            if zz > 0:
                drain(LEFT, 4 - zz, 7 * CS)

    drain(YN, 21, CS)

    @pl.when(c == 0)
    def _():
        drain(SIB, 14, GR)
        for a in range(14, 16):
            core_send(a, 0).wait_send()

    @pl.when(c == 1)
    def _():
        drain(SIB, 14, 2 * GR)
        drain(XN, 14, GR)
        for a in range(14, 16):
            core_send(a, 1).wait_send()
        for a in range(12, 16):
            for j in range(3):
                x_send(a, j).wait_send()

    for j in range(3):
        for a in (12, 14):
            y_send(a, 0, j).wait_send()
        for a in (11, 13):
            z_send(a, 0, j).wait_send()


PIECES = 3


def hand_over(blk, ig, fs, g1, g2, bsum, o_blk, o_ig, o_fs, o_g1, o_g2, o_b1, o_b2, wide, tall, sem):
    loads, stores = [], []
    for n, (src, dst) in enumerate(((blk, o_blk), (ig, o_ig), (fs, o_fs), (g1, o_g1), (g2, o_g2))):
        rows = src.shape[0] // PIECES
        for p in range(PIECES):
            at = pl.ds(p * rows, rows)
            held = wide.at[n, at] if n < 3 else tall.at[n - 3, at]
            loads.append(pltpu.make_async_copy(src.at[at], held, sem.at[0, n, p]))
            stores.append(pltpu.make_async_copy(held, dst.at[at], sem.at[1, n, p]))
            loads[-1].start()
    w = lax.axis_index("wide")
    for s in range(NW):

        @pl.when(w == s)
        def _(s=s):
            o_b1[...] = bsum[0:1, s * CS : (s + 1) * CS]
            o_b2[...] = bsum[8:9, s * CS : (s + 1) * CS]

    for load, store in zip(loads, stores):
        load.wait()
        store.start()
    for store in stores:
        store.wait()


def kernel_local(real_images, replay_chains, langevin_noise, real_cot, chain_cot, kernel_one, bias_one, kernel_two, bias_two):
    def flat(values):
        return values.reshape(values.shape[:-4] + (PX, C))

    anywhere = pl.BlockSpec(memory_space=pl.ANY)
    dma = pltpu.SemaphoreType.DMA
    out_shape = [jax.ShapeDtypeStruct((PX, C), F32)] * 3 + [jax.ShapeDtypeStruct((RS, C), F32)] * 2
    out_shape += [jax.ShapeDtypeStruct((16, C), F32)]
    scratch = [
        pltpu.VMEM((2 * NW * RS, C), BF16),
        pltpu.VMEM((2, PX, C), BF16),
        pltpu.VMEM((2, C, PX), BF16),
        pltpu.VMEM((2, C, PX), BF16),
        pltpu.VMEM((C, PX), BF16),
        pltpu.VMEM((2, C, PX), BF16),
        pltpu.VMEM((2 * C, PX), F32),
        pltpu.VMEM((2, C, PX), F32),
        pltpu.VMEM((2, C, PX), BF16),
        pltpu.VMEM((2, C, PX), BF16),
        pltpu.VMEM((PX // 256, NW * RS, 256), BF16),
        pltpu.VMEM((RS, 256), F32),
        pltpu.VMEM((2, RS, C), F32),
        pltpu.VMEM((PX, C), F32),
        pltpu.VMEM((2, C, LT), F32),
        pltpu.VMEM((NW, 8, LT), F32),
        pltpu.VMEM((10, 16, C), F32),
        pltpu.VMEM((2, 2 * GR, C), BF16),
        pltpu.VMEM((XSLOTS, GR, C), BF16),
        pltpu.VMEM((4, GR, C), BF16),
        pltpu.VMEM((2, GR, C), BF16),
        pltpu.VMEM((2 * GR, C), BF16),
        pltpu.VMEM((2, 2 * GR, C), BF16),
        pltpu.VMEM((2, GR, C), BF16),
        pltpu.VMEM((2, GR, C), BF16),
        pltpu.VMEM((GR, C), BF16),
        dma((2,)), dma((4,)), dma, dma((NW,)), dma((NW,)), dma((5,)), dma((2, NW, 9)),
        dma((2,)), dma((2,)), dma((4, 3)), dma((XSLOTS, 3)), dma((2, 3)), dma((4, 3)), dma((2, 3)), dma((2, 3, 3)),
        dma((2, 3)), dma((2, 3)), dma((2, 2, 3)), dma((2, 2, 3)), dma((6,)), dma((6,)),
    ]
    made = pl.pallas_call(
        body,
        out_shape=out_shape,
        in_specs=[anywhere] * 7 + [pl.BlockSpec(memory_space=pltpu.VMEM)] * 2,
        out_specs=[anywhere] * 6,
        scratch_shapes=scratch,
        compiler_params=pltpu.CompilerParams(
            collective_id=0, has_side_effects=True, vmem_limit_bytes=65400 * 2**10
        ),
    )(
        flat(real_images), flat(replay_chains), flat(langevin_noise), flat(real_cot), flat(chain_cot),
        kernel_one.reshape(RS, C), kernel_two.reshape(RS, C), bias_one.reshape(1, CS), bias_two.reshape(1, CS),
    )
    blk, ig, fs, g1, g2, first_bias, second_bias = pl.pallas_call(
        hand_over,
        out_shape=out_shape[:5] + [jax.ShapeDtypeStruct((1, CS), F32)] * 2,
        in_specs=[anywhere] * 5 + [pl.BlockSpec(memory_space=pltpu.VMEM)],
        out_specs=[anywhere] * 5 + [pl.BlockSpec(memory_space=pltpu.VMEM)] * 2,
        scratch_shapes=[pltpu.VMEM((3, PX, C), F32), pltpu.VMEM((2, RS, C), F32), dma((2, 5, PIECES))],
    )(*made)
    shape = real_images.shape
    return (
        blk.reshape(shape), ig.reshape(shape), fs.reshape(shape),
        g1.reshape(kernel_one.shape), first_bias.reshape(CS),
        g2.reshape(kernel_two.shape), second_bias.reshape(CS),
    )


def solution(mesh):
    def local(real_images, *rest):
        kernel_one = rest[4]
        fits = (
            mesh.shape["dp"] == 4
            and mesh.shape["wide"] == NW
            and real_images.shape == (12, 8, 8, C)
            and kernel_one.shape == (3, 3, CS, C)
            and rest[1].shape[0] == 2
        )
        return (kernel_local if fits else plain_local)(real_images, *rest)

    return jax.shard_map(
        local,
        mesh=mesh,
        in_specs=(
            P(("dp", "wide"), None, None, None),
            P(("dp", "wide"), None, None, None),
            P(None, ("dp", "wide"), None, None, None),
            P(("dp", "wide"), None, None, None),
            P(("dp", "wide"), None, None, None),
            P(None, None, "wide", None),
            P("wide"),
            P(None, None, "wide", None),
            P("wide"),
        ),
        out_specs=(
            P(("dp", "wide"), None, None, None),
            P(("dp", "wide"), None, None, None),
            P(("dp", "wide"), None, None, None),
            P(None, None, "wide", None),
            P("wide"),
            P(None, None, "wide", None),
            P("wide"),
        ),
        check_vma=False,
    )
```
